32 devices in a mesh: dp: 4 (over z), seq: 8 (over y, x, core).
Axes of the slice: x: 2, y: 2, z: 4, core: 2. Of those that a mesh axis runs over, the one named last changes fastest.
Arguments:
- tokens: bfloat16 [4, 1024, 1024], P('dp', 'seq'), may hold values from -6 to 6
- lengths: int32 [4], P('dp'), may hold values from 896 to 1024, as said below
- cotangent: bfloat16 [4, 1024, 1024], P('dp', 'seq'), may hold values from -6 to 6
- attention_weights: bfloat16 [3, 1024, 1024], P(None, ('dp', 'seq')), may hold values from -0.1875 to 0.1875
- output_weight: bfloat16 [1024, 1024], P(('dp', 'seq')), may hold values from -0.25 to 0.25
- decay_down_matrix: bfloat16 [1024, 64], P(('dp', 'seq')), may hold values from -0.1875 to 0.1875
- decay_up_matrix: bfloat16 [64, 1024], P(None, ('dp', 'seq')), may hold values from -0.75 to 0.75
- rate_down_matrix: bfloat16 [1024, 64], P(('dp', 'seq')), may hold values from -0.1875 to 0.1875
- rate_up_matrix: bfloat16 [64, 1024], P(None, ('dp', 'seq')), may hold values from -0.75 to 0.75
- gate_down_matrix: bfloat16 [1024, 128], P(('dp', 'seq')), may hold values from -0.1875 to 0.1875
- gate_up_matrix: bfloat16 [128, 1024], P(None, ('dp', 'seq')), may hold values from -0.5 to 0.5
- feedforward_key: bfloat16 [1024, 4096], P(('dp', 'seq')), may hold values from -0.1875 to 0.1875
- feedforward_value: bfloat16 [4096, 1024], P(('dp', 'seq')), may hold values from -0.09375 to 0.09375
- layer_norm_gains: bfloat16 [3, 1024], P(None, ('dp', 'seq')), may hold values from 0.5 to 1.5
- layer_norm_biases: bfloat16 [3, 1024], P(None, ('dp', 'seq')), may hold values from -1.5 to 1.5
- shift_coefficients: bfloat16 [7, 1024], P(None, ('dp', 'seq')), may hold values from 0 to 1
- decay_offset_base: bfloat16 [1024], P(('dp', 'seq')), may hold values from -8 to -1
- rate_logit_base: bfloat16 [1024], P(('dp', 'seq')), may hold values from -6 to 0
- removal_key_scales: bfloat16 [2, 1024], P(None, ('dp', 'seq')), may hold values from 0.5 to 1.5
- own_term_weights: bfloat16 [1024], P(('dp', 'seq')), may hold values from -0.29882812 to 0.29882812
Outputs:
- output: bfloat16 [4, 1024, 1024], P('dp', 'seq')
- input_grad: bfloat16 [4, 1024, 1024], P('dp', 'seq')
- grad_mix_weights: float32 [3, 1024, 1024], P(None, ('dp', 'seq'))
- grad_out_weight: float32 [1024, 1024], P(('dp', 'seq'))
- grad_decay_down: float32 [1024, 64], P(('dp', 'seq'))
- decay_up_gradient: float32 [64, 1024], P(None, ('dp', 'seq'))
- grad_rate_down: float32 [1024, 64], P(('dp', 'seq'))
- rate_up_gradient: float32 [64, 1024], P(None, ('dp', 'seq'))
- grad_gate_down: float32 [1024, 128], P(('dp', 'seq'))
- grad_gate_up: float32 [128, 1024], P(None, ('dp', 'seq'))
- grad_ffn_key: float32 [1024, 4096], P(('dp', 'seq'))
- grad_ffn_value: float32 [4096, 1024], P(('dp', 'seq'))
- grad_norm_gains: float32 [3, 1024], P(None, ('dp', 'seq'))
- grad_norm_biases: float32 [3, 1024], P(None, ('dp', 'seq'))
- grad_mix_coefs: float32 [6, 1024], P(None, ('dp', 'seq'))
- grad_decay_shift: float32 [1024], P(('dp', 'seq'))
- grad_decay_base: float32 [1024], P(('dp', 'seq'))
- grad_rate_base: float32 [1024], P(('dp', 'seq'))
- grad_key_scales: float32 [2, 1024], P(None, ('dp', 'seq'))
- grad_bonus_weights: float32 [1024], P(('dp', 'seq'))
The draws below stay inside these ranges and needn't reach their ends.
Inputs may be any that keep to these rules, and one draw needn't show every extreme that they name: `lengths`: each slot holds one sequence starting at its position 0; some slot is full (1024) and some has exactly min(1024, 896).
All inputs are finite; a program needn't handle non-finite values.
Results may differ from the reference program's by a relative error of at most 0.025.
Values may be sent and summed in bfloat16 or wider, within the bound.
No kernel may reach another device: no remote copies, remote signals or barrier semaphores. Data moves between devices by JAX's collectives and lax.ppermute only.
A program may use at most 192 MiB of HBM per device.

```python
import jax
import jax.numpy as jnp
from jax import lax

MODEL_WIDTH = 1024
FF = 4096
HEAD_SIZE = 64
DECAY_RANK = 64
RATE_RANK = 64
GATE_RANK = 128
BLOCK = 128
LEN_MIN = 1024
HEADS = 16
SLOT_LEN = 1024
SLOTS = 4


def draw_lengths(key, part):
    split_keys = jax.random.split(jax.random.fold_in(key, 11), 3)
    low_end = min(LEN_MIN, SLOT_LEN - BLOCK)
    drawn = jax.random.randint(split_keys[0], (SLOTS,), low_end, SLOT_LEN + 1)
    full_slot = jax.random.randint(split_keys[1], (), 0, SLOTS)
    short_slot = (full_slot + 1 + jax.random.randint(split_keys[2], (), 0, SLOTS - 1)) % SLOTS
    drawn = drawn.at[full_slot].set(SLOT_LEN)
    drawn = drawn.at[short_slot].set(low_end)
    return drawn.astype(jnp.int32)


def block_scale(own_key, shape, shards, smallest, largest):
    def one(dim, blocks):
        heights = jax.random.uniform(jax.random.fold_in(jax.random.fold_in(own_key, 6), dim), (blocks,), jnp.float32, smallest / len(shards), largest / len(shards))
        return jnp.repeat(jnp.exp(heights), shape[dim] // blocks).reshape((-1,) + (1,) * (len(shape) - dim - 1))

    loudness = one(*shards[0])
    for cut in shards[1:]:
        loudness = loudness * one(*cut)
    return loudness


def scatter_about(rng, dims, scale, reach, pieces=(), kind=jnp.bfloat16):
    result = jax.random.normal(rng, dims, jnp.float32) * scale
    if len(pieces) > 0:
        result = block_scale(rng, dims, pieces, -0.22, 0.18) * result
    return jnp.clip(result, min=-reach, max=reach).astype(kind)


def setup_inputs(seed: int = 0) -> dict:
    arg_keys = jax.random.split(jax.random.key(seed), 21)
    tokens = scatter_about(arg_keys[0], (SLOTS, SLOT_LEN, MODEL_WIDTH), 1.0, 6.0, ((0, 4), (1, 8)))
    lengths = draw_lengths(jax.random.fold_in(arg_keys[20], 71), 0)
    cotangent = scatter_about(arg_keys[2], (SLOTS, SLOT_LEN, MODEL_WIDTH), 1.0, 6.0, ((0, 4), (1, 8)))
    attention_weights = scatter_about(arg_keys[3], (3, MODEL_WIDTH, MODEL_WIDTH), MODEL_WIDTH ** -0.5, 0.1875, ((1, 32),))
    output_weight = scatter_about(arg_keys[4], (MODEL_WIDTH, MODEL_WIDTH), (MODEL_WIDTH // 2) ** -0.5, 0.25, ((0, 32),))
    decay_down_matrix = scatter_about(arg_keys[5], (MODEL_WIDTH, DECAY_RANK), MODEL_WIDTH ** -0.5, 0.1875, ((0, 32),))
    decay_up_matrix = scatter_about(arg_keys[6], (DECAY_RANK, MODEL_WIDTH), DECAY_RANK ** -0.5, 0.75, ((1, 32),))
    rate_down_matrix = scatter_about(arg_keys[7], (MODEL_WIDTH, RATE_RANK), MODEL_WIDTH ** -0.5, 0.1875, ((0, 32),))
    rate_up_matrix = scatter_about(arg_keys[8], (RATE_RANK, MODEL_WIDTH), RATE_RANK ** -0.5, 0.75, ((1, 32),))
    gate_down_matrix = scatter_about(arg_keys[9], (MODEL_WIDTH, GATE_RANK), MODEL_WIDTH ** -0.5, 0.1875, ((0, 32),))
    gate_up_matrix = scatter_about(arg_keys[10], (GATE_RANK, MODEL_WIDTH), GATE_RANK ** -0.5, 0.5, ((1, 32),))
    feedforward_key = scatter_about(arg_keys[11], (MODEL_WIDTH, FF), MODEL_WIDTH ** -0.5, 0.1875, ((0, 32),))
    feedforward_value = scatter_about(arg_keys[12], (FF, MODEL_WIDTH), FF ** -0.5, 0.09375, ((0, 32),))
    layer_norm_gains = jnp.clip(1.0 + 0.1 * jax.random.normal(arg_keys[13], (3, MODEL_WIDTH), jnp.float32), 0.5, 1.5).astype(jnp.bfloat16)
    layer_norm_biases = scatter_about(arg_keys[14], (3, MODEL_WIDTH), 0.3, 1.5, ((1, 32),))
    shift_coefficients = jnp.clip(1.0 * jax.random.uniform(arg_keys[15], (7, MODEL_WIDTH), jnp.float32) ** block_scale(arg_keys[15], (7, MODEL_WIDTH), ((1, 32),), -0.2, 0.2), 0.0, 1.0).astype(jnp.bfloat16)
    decay_offset_base = jnp.clip(-8.0 + 7.0 * jax.random.uniform(arg_keys[16], (MODEL_WIDTH,), jnp.float32) ** block_scale(arg_keys[16], (MODEL_WIDTH,), ((0, 32),), -0.2, 0.2), -8.0, -1.0).astype(jnp.bfloat16)
    rate_logit_base = jnp.clip(-6.0 + 6.0 * jax.random.uniform(arg_keys[17], (MODEL_WIDTH,), jnp.float32) ** block_scale(arg_keys[17], (MODEL_WIDTH,), ((0, 32),), -0.2, 0.2), -6.0, 0.0).astype(jnp.bfloat16)
    removal_key_scales = jnp.clip(1.0 + 0.1 * jax.random.normal(arg_keys[18], (2, MODEL_WIDTH), jnp.float32), 0.5, 1.5).astype(jnp.bfloat16)
    own_term_weights = scatter_about(arg_keys[19], (MODEL_WIDTH,), 0.05, 0.29882812, ((0, 32),))
    return {"tokens": tokens, "lengths": lengths, "cotangent": cotangent, "attention_weights": attention_weights, "output_weight": output_weight, "decay_down_matrix": decay_down_matrix, "decay_up_matrix": decay_up_matrix, "rate_down_matrix": rate_down_matrix, "rate_up_matrix": rate_up_matrix, "gate_down_matrix": gate_down_matrix, "gate_up_matrix": gate_up_matrix, "feedforward_key": feedforward_key, "feedforward_value": feedforward_value, "layer_norm_gains": layer_norm_gains, "layer_norm_biases": layer_norm_biases, "shift_coefficients": shift_coefficients, "decay_offset_base": decay_offset_base, "rate_logit_base": rate_logit_base, "removal_key_scales": removal_key_scales, "own_term_weights": own_term_weights}


HIGH = lax.Precision.HIGHEST
LN_EPS = 1e-05
GN_EPS = 0.00064
NORM_EPS = 1e-06

@jax.custom_vjp
def low(v):
    return lax.optimization_barrier(v.astype(jnp.bfloat16)).astype(jnp.float32)

@jax.custom_vjp
def low_back(v):
    return v

def low_keep(v):
    return (low(v), None)

def low_pass(kept, grad):
    return (grad,)

def back_keep(v):
    return (v, None)

def back_low(kept, grad):
    return (low(grad),)
low.defvjp(low_keep, low_pass)
low_back.defvjp(back_keep, back_low)

def matrix_multiply(left, right):
    return jnp.dot(left, right, precision=HIGH, preferred_element_type=jnp.float32)

def layer_norm(content_entries, gain, bias):
    center = content_entries - lax.optimization_barrier(jnp.mean(content_entries, -1, keepdims=True))
    spread = lax.optimization_barrier(jnp.mean(center * center, -1, keepdims=True))
    return center * lax.rsqrt(spread + LN_EPS) * gain + bias

def shifted(content_entries):
    return jnp.concatenate([jnp.zeros_like(content_entries[:1]), content_entries[:-1]], 0)

def prepare_inputs(unscaled_keys, decay_adapter, rate_adapter, fading_displacement_intercept, pace_displacement_intercept, lookup_scalar):
    logarithm_rate = -jax.nn.softplus(-(fading_displacement_intercept + decay_adapter)) - 0.5
    decay_speed = jnp.exp(-jnp.exp(logarithm_rate))
    rate_activation = jax.nn.sigmoid(pace_displacement_intercept + rate_adapter)
    subspace_arrangement = unscaled_keys.shape[:-1] + (HEADS, HEAD_SIZE)
    scaled = (unscaled_keys * lookup_scalar[0]).reshape(subspace_arrangement)
    removal_key_unit = scaled * lax.rsqrt(lax.optimization_barrier(jnp.sum(scaled * scaled, -1, keepdims=True)) + NORM_EPS)
    closing_lookup_vectors = unscaled_keys * (1.0 + (rate_activation - 1.0) * lookup_scalar[1])
    removal_key_rate = removal_key_unit * rate_activation.reshape(subspace_arrangement)
    return (decay_speed.reshape(subspace_arrangement), closing_lookup_vectors.reshape(subspace_arrangement), removal_key_unit, removal_key_rate)

def combined_result(emitted_entries, acceptor_entries, closing_lookup_vectors, content_entries, valve_response, extra_reward_scalar, cluster_standardize_amplifier, cluster_standardize_intercept):
    subspace_arrangement = emitted_entries.shape
    center = emitted_entries - lax.optimization_barrier(jnp.mean(emitted_entries, -1, keepdims=True))
    spread = lax.optimization_barrier(jnp.mean(center * center, -1, keepdims=True))
    standardized_entries = (center * lax.rsqrt(spread + GN_EPS)).reshape(valve_response.shape) * cluster_standardize_amplifier + cluster_standardize_intercept
    acceptor_subspaces = acceptor_entries.reshape(subspace_arrangement)
    extra_reward_aggregate = lax.optimization_barrier(jnp.sum(acceptor_subspaces * closing_lookup_vectors * extra_reward_scalar.reshape(subspace_arrangement[-2:]), -1, keepdims=True))
    return (standardized_entries + (extra_reward_aggregate * content_entries.reshape(subspace_arrangement)).reshape(valve_response.shape)) * valve_response

def recur(acceptor_entries, decay_speed, closing_lookup_vectors, content_entries, removal_key_unit, removal_key_rate):
    length = acceptor_entries.shape[0]

    def token_step(state_now, inputs):
        rec_vec, dec_vec, key_vec, val_vec, unit_vec, rate_vec = inputs
        removed = jnp.einsum('hij,hj->hi', state_now, unit_vec, precision=HIGH)
        state_now = state_now * dec_vec[:, None, :] - removed[:, :, None] * rate_vec[:, None, :] + val_vec[:, :, None] * key_vec[:, None, :]
        return (state_now, jnp.einsum('hij,hj->hi', state_now, rec_vec, precision=HIGH))

    def block_step(state_now, inputs):
        return lax.scan(token_step, state_now, inputs)
    members = (acceptor_entries, decay_speed, closing_lookup_vectors, content_entries, removal_key_unit, removal_key_rate)
    stacked = tuple((tree_element.reshape(length // 64, 64, HEADS, HEAD_SIZE) for tree_element in members))
    initial = jnp.zeros((HEADS, HEAD_SIZE, HEAD_SIZE), jnp.float32)
    final_state, emitted_entries = lax.scan(jax.checkpoint(block_step), initial, stacked)
    return emitted_entries.reshape(length, HEADS, HEAD_SIZE)

def forward(trainable_settings, tokens, valid_mask):
    combining_linear_map, emitted_linear_map, fading_entering_signal, fading_result_signal, pace_entering_signal, pace_result_signal, valve_entering_signal, valve_result_signal, channel_mixer_entering, channel_mixer_result, standardize_amplifier, standardize_intercept, displacement_scalar, fading_displacement_intercept, pace_displacement_intercept, lookup_scalar, extra_reward_scalar = trainable_settings
    standardized_entries = layer_norm(tokens, standardize_amplifier[0], standardize_intercept[0])
    delta = shifted(standardized_entries) - standardized_entries
    recep_mix, decay_blend, key_mix, value_mix, rate_blend, gate_mix = [low(standardized_entries + delta * displacement_scalar[coef_index]) for coef_index in range(6)]
    acceptor_entries = low_back(matrix_multiply(recep_mix, combining_linear_map[0]))
    unscaled_keys = low_back(matrix_multiply(key_mix, combining_linear_map[1]))
    content_entries = low_back(matrix_multiply(value_mix, combining_linear_map[2]))
    decay_adapter = low_back(matrix_multiply(low(jnp.tanh(low_back(matrix_multiply(decay_blend, fading_entering_signal)))), fading_result_signal))
    rate_adapter = low_back(matrix_multiply(low(low_back(matrix_multiply(rate_blend, pace_entering_signal))), pace_result_signal))
    valve_response = low_back(matrix_multiply(low(jax.nn.sigmoid(low_back(matrix_multiply(gate_mix, valve_entering_signal)))), valve_result_signal))
    decay_speed, closing_lookup_vectors, removal_key_unit, removal_key_rate = prepare_inputs(unscaled_keys, decay_adapter, rate_adapter, fading_displacement_intercept, pace_displacement_intercept, lookup_scalar)
    emitted_entries = recur(acceptor_entries, decay_speed, closing_lookup_vectors, content_entries, removal_key_unit, removal_key_rate)
    narrow_context_adaptor = low(combined_result(emitted_entries, acceptor_entries, closing_lookup_vectors, content_entries, valve_response, extra_reward_scalar, standardize_amplifier[2], standardize_intercept[2]))
    resid = tokens + low_back(matrix_multiply(narrow_context_adaptor, emitted_linear_map))
    normed_ffn = layer_norm(resid, standardize_amplifier[1], standardize_intercept[1])
    ffn_mix = low(normed_ffn + (shifted(normed_ffn) - normed_ffn) * displacement_scalar[6])
    ffn_hidden = low_back(matrix_multiply(ffn_mix, channel_mixer_entering))
    ffn_act = low(jnp.square(jax.nn.relu(ffn_hidden)))
    ffn_result = low_back(matrix_multiply(ffn_act, channel_mixer_result))
    return valid_mask[:, None] * (resid + ffn_result)

def reference(tokens, lengths, cotangent, attention_weights, output_weight, decay_down_matrix, decay_up_matrix, rate_down_matrix, rate_up_matrix, gate_down_matrix, gate_up_matrix, feedforward_key, feedforward_value, layer_norm_gains, layer_norm_biases, shift_coefficients, decay_offset_base, rate_logit_base, removal_key_scales, own_term_weights):
    trainable_settings = tuple((tree_element.astype(jnp.float32) for tree_element in (attention_weights, output_weight, decay_down_matrix, decay_up_matrix, rate_down_matrix, rate_up_matrix, gate_down_matrix, gate_up_matrix, feedforward_key, feedforward_value, layer_norm_gains, layer_norm_biases, shift_coefficients, decay_offset_base, rate_logit_base, removal_key_scales, own_term_weights)))
    positions = jnp.arange(SLOT_LEN, dtype=jnp.int32)

    def per_slot(totals, slot_in):
        slot_tokens, slot_cot, slot_len = slot_in
        valid_mask = (positions < slot_len.astype(jnp.int32)).astype(jnp.float32)

        def run_slot(weights_now, inputs):
            return forward(weights_now, inputs, valid_mask)
        output, pullback = jax.vjp(run_slot, trainable_settings, slot_tokens.astype(jnp.float32))
        weight_grads, input_grad = pullback(slot_cot.astype(jnp.float32))
        totals = jax.tree.map(jnp.add, totals, weight_grads)
        return (totals, (output.astype(jnp.bfloat16), input_grad.astype(jnp.bfloat16)))
    zeros_init = tuple((jnp.zeros_like(tree_element) for tree_element in trainable_settings))
    totals, (emitted_entries, input_grads) = lax.scan(per_slot, zeros_init, (tokens, cotangent, lengths))
    coef_totals = totals[12]
    other_coefs = jnp.concatenate([coef_totals[:1], coef_totals[2:]], 0)
    return (emitted_entries, input_grads, totals[0], totals[1], totals[2], totals[3], totals[4], totals[5], totals[6], totals[7], totals[8], totals[9], totals[10], totals[11], other_coefs, coef_totals[1], totals[13], totals[14], totals[15], totals[16])
```

```python
from functools import partial

import jax
import jax.numpy as jnp
from jax import lax
from jax.experimental import pallas as pl
from jax.experimental.pallas import tpu as pltpu
from jax.sharding import PartitionSpec as P

HEAD_SIZE = 64
HEADS = 16
BOTH = ("dp", "seq")

HIGH = lax.Precision.HIGHEST
LN_EPS = 1e-05
GN_EPS = 0.00064
NORM_EPS = 1e-06
F32 = jnp.float32
BF = jnp.bfloat16
PASSES = 3


def shifted(value, axis, steps):
    count = lax.axis_size(axis)
    first, last = (max(0, -steps), min(count, count - steps))
    return lax.ppermute(value, axis, [(source, source + steps) for source in range(first, last)])


def layer_norm(content_entries, gain, bias):
    center = content_entries - jnp.mean(content_entries, -1, keepdims=True)
    spread = jnp.mean(center * center, -1, keepdims=True)
    return center * lax.rsqrt(spread + LN_EPS) * gain + bias


def token_mix(standardized_entries, left_edge, coefs):
    previous = jnp.concatenate([left_edge, standardized_entries[:, :-1]], 1)
    delta = previous - standardized_entries
    return tuple(
        (standardized_entries + delta * coefs[coef_index] for coef_index in range(coefs.shape[0]))
    )


def prepare_inputs(keys_raw, decay_lora, rate_lora, decay_base, rate_base, key_scales):
    log_decay = -jnp.exp(-jax.nn.softplus(-(decay_base + decay_lora)) - 0.5)
    rate = jax.nn.sigmoid(rate_base + rate_lora)
    scaled = (keys_raw * key_scales[0]).reshape(keys_raw.shape[:-1] + (HEADS, HEAD_SIZE))
    unit = scaled * lax.rsqrt(jnp.sum(scaled * scaled, -1, keepdims=True) + NORM_EPS)
    unit = unit.reshape(keys_raw.shape)
    keys_fin = keys_raw * (1.0 + (rate - 1.0) * key_scales[1])
    return log_decay, keys_fin, unit, unit * rate


def combined_result(wkv, receptance, keys_fin, values, gate_value, own_weights, gain, bias):
    split = wkv.shape[:-1] + (HEADS, HEAD_SIZE)
    heads = wkv.reshape(split)
    center = heads - jnp.mean(heads, -1, keepdims=True)
    spread = jnp.mean(center * center, -1, keepdims=True)
    normed = (center * lax.rsqrt(spread + GN_EPS)).reshape(wkv.shape) * gain + bias
    own = jnp.sum((receptance * keys_fin * own_weights).reshape(split), -1, keepdims=True)
    return (normed + (own * values.reshape(split)).reshape(wkv.shape)) * gate_value


def dg(a,b,ca,cb):
    return lax.dot_general(a,b,(((ca,),(cb,)),((),())),preferred_element_type=F32)

def mm(a,b,ca=1,cb=0,passes=1):
    if passes==1:
        return dg(a.astype(BF),b.astype(BF),ca,cb)
    ah=a.astype(BF); bh=b.astype(BF)
    al=(a-ah.astype(F32)).astype(BF); bl=(b-bh.astype(F32)).astype(BF)
    return dg(ah,bh,ca,cb)+(dg(ah,bl,ca,cb)+dg(al,bh,ca,cb))

def iota(shape,d): return lax.broadcasted_iota(jnp.int32,shape,d)

def lanes(n):
    lane=iota((1,n),1)
    return (lane<n//2).astype(F32),(lane>=n//2).astype(F32)

def halves(x,m0,m1):
    return jnp.concatenate([x*m0,x*m1],0)

def compact(g,m0,m1):
    h=g.shape[0]//2
    return g[:h]*m0+g[h:]*m1

def scaled_inputs(r,k,kk,b,lw):
    n=lw.shape[0]
    tri=(iota((n,n),0)>=iota((n,n),1)).astype(F32)
    cum=lax.dot_general(tri,lw,(((1,),(0,)),((),())),precision=HIGH,preferred_element_type=F32)
    total=cum[n-1:n]
    center=0.5*total
    up=jnp.exp(cum-center)
    upx=jnp.exp(cum-lw-center)
    down=jnp.exp(center-cum)
    at=-kk*upx; rt=r*up; bt=b*down; kt=k*down
    return at,rt,bt,kt,center,total,up,upx,down

def score_mask(n):
    t=iota((2*n,2*n),0); s=iota((2*n,2*n),1)
    low=t<n
    tt=jnp.where(low,t,t-n); ss=jnp.where(s<n,s,s-n)
    return (ss<tt)|((ss==tt)&jnp.logical_not(low))

def invert(a,passes):
    n=a.shape[0]
    t=iota((n,n),0); s=iota((n,n),1)
    x=t^s
    inv=jnp.where(t==s,1.0,0.0)+jnp.where((x==1),a,0.0)
    b=2
    while b<n:
        off=jnp.where((x>=b)&(x<2*b),a,0.0)
        inv=inv+mm(inv,mm(off,inv,passes=passes),passes=passes)
        b*=2
    return inv

def fwd_pair(r,k,v,kk,b,lw,pt,p):
    n=r.shape[0]; m0,m1=lanes(r.shape[1])
    at,rt,bt,kt,center,total,*_=scaled_inputs(r,k,kk,b,lw)
    x=jnp.concatenate([at,rt],0); y=jnp.concatenate([bt,kt],0)
    mask=score_mask(n)
    s0=jnp.where(mask,mm(x*m0,y,1,1,p),0.0)
    s1=jnp.where(mask,mm(x*m1,y,1,1,p),0.0)
    t0=invert(s0[:n,:n],pt); t1=invert(s1[:n,:n],pt)
    vs=halves(v,m0,m1)
    akv=mm(jnp.concatenate([s0[:n,n:],s1[:n,n:]],1),vs,passes=p)
    t01=jnp.concatenate([t0,t1],1)
    w=mm(t01,halves(at,m0,m1),passes=p); uv=mm(t01,halves(akv,m0,m1),passes=p)
    rb=jnp.concatenate([s0[n:,:n],s1[n:,:n]],1); rk=jnp.concatenate([s0[n:,n:],s1[n:,n:]],1)
    q=rt+mm(rb,halves(w,m0,m1),passes=p)
    oloc=mm(rb,halves(uv,m0,m1),passes=p)+mm(rk,vs,passes=p)
    ec=jnp.exp(center); er=jnp.exp(total-center)
    q0=q*ec; w0=w*ec
    bh=bt*er; kh=kt*er
    dfull=mm(w0,bh,0,0,p); efull=mm(uv,bh,0,0,p)+mm(v,kh,0,0,p)
    half=r.shape[1]//2
    lane=iota((half,2*half),1); row=iota((half,2*half),0)
    eye=jnp.where((lane==row)|(lane==row+half),1.0,0.0)
    d=compact(dfull,m0,m1)+eye*jnp.exp(total)
    e=compact(efull,m0,m1)
    return q0,oloc,w0,uv,t01,d,e

def bwd_pair(r,k,v,kk,b,lw,t01,w0,uv,do,s_in,ds_out,p):
    n=r.shape[0]; m0,m1=lanes(r.shape[1])
    at,rt,bt,kt,center,total,up,upx,down=scaled_inputs(r,k,kk,b,lw)
    x=jnp.concatenate([at,rt],0); y=jnp.concatenate([bt,kt],0)
    mask=score_mask(n)
    s0=jnp.where(mask,mm(x*m0,y,1,1,p),0.0)
    s1=jnp.where(mask,mm(x*m1,y,1,1,p),0.0)
    ec=jnp.exp(center); er=jnp.exp(total-center)
    stil=halves(s_in*ec,m0,m1); sraw=halves(s_in,m0,m1); dst=halves(ds_out*er,m0,m1)
    u=mm(w0,sraw,1,1,p)+uv
    dos=halves(do,m0,m1)
    du=mm(jnp.concatenate([s0[n:,:n],s1[n:,:n]],0),dos,0,0,p)+mm(bt,dst,1,1,p)
    z=mm(jnp.concatenate([t01[:,:n],t01[:,n:]],0),halves(du,m0,m1),0,0,p)
    zo=jnp.concatenate([z,do],0)
    dv=mm(s0[:,n:],zo*m0,0,0,p)+mm(s1[:,n:],zo*m1,0,0,p)+mm(kt,dst,1,1,p)
    uvs=jnp.concatenate([u,v],0)
    g0=jnp.where(mask,mm(zo*m0,uvs,1,1,p),0.0)
    g1=jnp.where(mask,mm(zo*m1,uvs,1,1,p),0.0)
    dx=mm(g0,y*m0,passes=p)+mm(g1,y*m1,passes=p)+mm(zo,stil,passes=p)
    dy=mm(g0,x*m0,0,0,p)+mm(g1,x*m1,0,0,p)+mm(uvs,dst,passes=p)
    da=dx[:n]; dr=dx[n:]; db=dy[:n]; dk=dy[n:]
    if p==1:
        rnd=lambda q: q.astype(BF).astype(F32)
    else:
        rnd=lambda q:q
    gl=rnd(rt)*dr-rnd(bt)*db-rnd(kt)*dk
    ga=rnd(at)*da
    gend=jnp.sum(rnd(dst)*(stil+mm(u,bt,0,0,p)+mm(v,kt,0,0,p)),0,keepdims=True)
    tri=(iota((n,n),0)<=iota((n,n),1)).astype(F32)
    glw=lax.dot_general(tri,gl+ga,(((1,),(0,)),((),())),precision=HIGH,preferred_element_type=F32)-ga+gend
    return dr*up,dk*down,dv,-da*upx,db*down,glw

def fwd_kernel(pt,p,r,k,v,kk,b,lw,q0,oloc,w0,uv,t01,d,e):
    outs=fwd_pair(r[...],k[...],v[...],kk[...],b[...],lw[...],pt,p)
    for ref,val in zip((q0,oloc,w0,uv,t01,d,e),outs): ref[...]=val.astype(ref.dtype)

def bwd_kernel(p,*refs):
    outs=bwd_pair(*[q[...].astype(F32) for q in refs[:12]],p)
    for ref,val in zip(refs[12:],outs): ref[...]=val.astype(ref.dtype)


STATE = HEAD_SIZE
PAIR = 2 * HEAD_SIZE


def specs(rows):
    col = pl.BlockSpec((rows, PAIR), lambda i: (0, i))
    state = pl.BlockSpec((STATE, PAIR), lambda i: (0, i))
    wide = pl.BlockSpec((rows, 2 * rows), lambda i: (0, i))
    return col, state, wide


def rec_forward(*args):
    n, f = args[0].shape
    pairs = f // PAIR
    col, state, wide = specs(n)
    shape = jax.ShapeDtypeStruct
    return pl.pallas_call(
        partial(fwd_kernel, PASSES, PASSES),
        grid=(pairs,),
        in_specs=[col] * 6,
        out_specs=[col] * 4 + [wide, state, state],
        out_shape=[shape((n, f), F32)] * 4
        + [shape((n, pairs * 2 * n), F32)]
        + [shape((STATE, f), F32)] * 2,
        compiler_params=pltpu.CompilerParams(vmem_limit_bytes=48 << 20),
        name="rec_forward",
    )(*args)


def rec_backward(*args):
    n, f = args[0].shape
    pairs = f // PAIR
    col, state, wide = specs(n)
    return pl.pallas_call(
        partial(bwd_kernel, PASSES),
        grid=(pairs,),
        in_specs=[col] * 6 + [wide, col, col, col, state, state],
        out_specs=[col] * 6,
        out_shape=[jax.ShapeDtypeStruct((n, f), F32)] * 6,
        compiler_params=pltpu.CompilerParams(vmem_limit_bytes=48 << 20),
        name="rec_backward",
    )(*args)


def combine_kernel(side, dl_ref, el_ref, d_ref, e_ref, dn_ref, en_ref):
    m0, m1 = lanes(PAIR)
    for pair in range(d_ref.shape[1] // PAIR):
        cols = pl.ds(pair * PAIR, PAIR)
        dl = dl_ref[:, cols].astype(F32)
        el = el_ref[:, cols].astype(F32)
        d = d_ref[:, cols]
        block = halves(d, m0, m1)
        if side == 1:
            both = mm(jnp.concatenate([dl, el], 0), block, passes=PASSES)
            dn_ref[:, cols] = both[:STATE]
            en_ref[:, cols] = both[STATE:] + e_ref[:, cols]
        else:
            en_ref[:, cols] = mm(el, block, 1, 1, passes=PASSES) + e_ref[:, cols]
            right = halves(dl, m0, m1)
            dn_ref[:, cols] = mm(d, right, passes=PASSES)


def combine(side, dl, el, d, e):
    return pl.pallas_call(
        partial(combine_kernel, side),
        out_shape=[jax.ShapeDtypeStruct(d.shape, F32)] * 2,
        compiler_params=pltpu.CompilerParams(vmem_limit_bytes=32 << 20),
        name="combine_states",
    )(dl, el, d, e)


def scan_states(transfer, offset, side):
    count = lax.axis_size("seq")

    def move(value, steps):
        return shifted(value.astype(BF), "seq", side * steps)

    d, e = move(transfer, 1).astype(F32), move(offset, 1).astype(F32)
    reach = 1
    while reach < count - 1:
        d, e = combine(side, move(d, reach), move(e, reach), d, e)
        reach *= 2
    return e


def apply_state_kernel(q_ref, s_ref, o_ref, out_ref):
    m0, m1 = lanes(PAIR)
    for pair in range(q_ref.shape[1] // PAIR):
        cols = pl.ds(pair * PAIR, PAIR)
        block = halves(s_ref[:, cols], m0, m1)
        out_ref[:, cols] = o_ref[:, cols] + mm(q_ref[:, cols], block, 1, 1, passes=PASSES)


def apply_state(q, s, o):
    return pl.pallas_call(
        apply_state_kernel,
        out_shape=jax.ShapeDtypeStruct(q.shape, F32),
        compiler_params=pltpu.CompilerParams(vmem_limit_bytes=32 << 20),
        name="apply_state",
    )(q, s, o)


def back_offset_kernel(do_ref, q_ref, f_ref):
    m0, m1 = lanes(PAIR)
    for pair in range(q_ref.shape[1] // PAIR):
        cols = pl.ds(pair * PAIR, PAIR)
        f_ref[:, cols] = compact(mm(do_ref[:, cols], q_ref[:, cols], 0, 0, PASSES), m0, m1)


def back_offset(do, q):
    return pl.pallas_call(
        back_offset_kernel,
        out_shape=jax.ShapeDtypeStruct((STATE, q.shape[1]), F32),
        compiler_params=pltpu.CompilerParams(vmem_limit_bytes=32 << 20),
        name="back_offset",
    )(do, q)

def input_backward(gradient, weight):
    return lax.dot_general(
        gradient, weight, (((1,), (1,)), ((), ())), preferred_element_type=jnp.float32
    )


def weight_backward(inputs, gradient):
    return lax.dot_general(
        inputs, gradient, (((0,), (0,)), ((), ())), preferred_element_type=jnp.float32
    )


def project(inputs, weight):
    return jnp.dot(inputs, weight, preferred_element_type=jnp.float32)


def gather_rows(packed):
    return lax.all_gather(packed, BOTH, axis=0, tiled=False)


def scatter_rows(packed):
    dp, seq = lax.axis_size("dp"), lax.axis_size("seq")
    packed = packed.reshape((dp, seq) + packed.shape[1:])
    over_seq = lax.psum_scatter(packed, "seq", scatter_dimension=1, tiled=False)
    return lax.psum_scatter(over_seq, "dp", scatter_dimension=0, tiled=False)


def as_rows(flat, width):
    rows = -(-flat.shape[-1] // width)
    padding = [(0, 0)] * (flat.ndim - 1) + [(0, rows * width - flat.shape[-1])]
    return jnp.pad(flat, padding).reshape(flat.shape[:-1] + (rows, width))


def local(
    tokens,
    lengths,
    cotangent,
    attention_weights,
    output_weight,
    decay_down_matrix,
    decay_up_matrix,
    rate_down_matrix,
    rate_up_matrix,
    gate_down_matrix,
    gate_up_matrix,
    feedforward_key,
    feedforward_value,
    layer_norm_gains,
    layer_norm_biases,
    shift_coefficients,
    decay_offset_base,
    rate_logit_base,
    removal_key_scales,
    own_term_weights,
):
    slot_count, block_len, width = tokens.shape
    rows = slot_count * block_len
    own = output_weight.shape[0]
    devices = width // own
    ranks = (decay_down_matrix.shape[1], rate_down_matrix.shape[1], gate_down_matrix.shape[1])
    low = sum(ranks)
    cut0, cut1 = ranks[0], ranks[0] + ranks[1]

    downs = jnp.concatenate([decay_down_matrix, rate_down_matrix, gate_down_matrix], 1)
    ups = jnp.concatenate([decay_up_matrix, rate_up_matrix, gate_up_matrix], 0)
    vectors = jnp.concatenate(
        [
            layer_norm_gains,
            layer_norm_biases,
            shift_coefficients,
            decay_offset_base[None],
            rate_logit_base[None],
            removal_key_scales,
            own_term_weights[None],
        ],
        0,
    )
    vector_count = vectors.shape[0]
    small = as_rows(
        jnp.concatenate([downs.reshape(-1), ups.reshape(-1), vectors.reshape(-1)]), width
    )
    packed = jnp.concatenate([attention_weights.reshape(-1, width), output_weight, small], 0)
    gathered = gather_rows(packed)
    weight_r, weight_k, weight_v, weight_o = [
        gathered[:, j * own : (j + 1) * own].reshape(width, width) for j in range(4)
    ]
    rest = gathered[:, 4 * own :].reshape(devices, -1)
    down = rest[:, : own * low].reshape(width, low)
    up = jnp.moveaxis(rest[:, own * low : 2 * own * low].reshape(devices, low, own), 0, 1)
    up = up.reshape(low, width)
    vecs = rest[:, 2 * own * low :][:, : vector_count * own].reshape(devices, vector_count, own)
    vecs = jnp.moveaxis(vecs, 0, 1).reshape(vector_count, width).astype(F32)
    gains, biases, coefs = vecs[:3], vecs[3:6], vecs[6:13]
    decay_base, rate_base, key_scales, own_weights = vecs[13], vecs[14], vecs[15:17], vecs[17]
    ffn_key = lax.all_gather(feedforward_key, BOTH, axis=0, tiled=True)
    ffn_value = lax.all_gather(feedforward_value, BOTH, axis=0, tiled=True)

    first_pos = lax.axis_index("seq") * block_len
    positions = first_pos + jnp.arange(block_len, dtype=jnp.int32)
    valid_mask = (positions[None, :] < lengths[:, None]).astype(jnp.float32)[:, :, None]
    inputs = tokens.astype(jnp.float32)
    normed, norm_pull = jax.vjp(layer_norm, inputs, gains[0], biases[0])
    left_edge = shifted(normed[:, -1:], "seq", 1)
    mixed_rows, mix_pull = jax.vjp(token_mix, normed, left_edge, coefs[:6])
    recep_mix, decay_mix, key_mix, value_mix, rate_mix, gate_mix = [
        item.reshape(rows, width).astype(BF) for item in mixed_rows
    ]
    receptance = project(recep_mix, weight_r)
    keys_raw = project(key_mix, weight_k)
    values = project(value_mix, weight_v)
    decay_tanh = jnp.tanh(project(decay_mix, down[:, :cut0]))
    decay_hidden = decay_tanh.astype(BF)
    decay_lora = project(decay_hidden, up[:cut0])
    rate_hidden = project(rate_mix, down[:, cut0:cut1]).astype(BF)
    rate_lora = project(rate_hidden, up[cut0:cut1])
    gate_sig = jax.nn.sigmoid(project(gate_mix, down[:, cut1:]))
    gate_low = gate_sig.astype(BF)
    gate_value = project(gate_low, up[cut1:])
    prepared, prep_pull = jax.vjp(
        prepare_inputs, keys_raw, decay_lora, rate_lora, decay_base, rate_base, key_scales
    )
    log_decay, keys_fin, unit, unit_rate = prepared
    streams = (receptance, keys_fin, values, unit, unit_rate, log_decay)
    q0, o_local, w0, uv, inverse, transfer, offset = rec_forward(*streams)
    state_in = scan_states(transfer, offset, 1)
    wkv = apply_state(q0, state_in, o_local)
    attn_pre, combine_pull = jax.vjp(
        combined_result,
        wkv,
        receptance,
        keys_fin,
        values,
        gate_value,
        own_weights,
        gains[2],
        biases[2],
    )
    attn_in = attn_pre.astype(BF)
    resid = inputs + project(attn_in, weight_o).reshape(inputs.shape)
    normed_ffn, norm_ffn_pull = jax.vjp(layer_norm, resid, gains[1], biases[1])
    ffn_edge = shifted(normed_ffn[:, -1:], "seq", 1)
    ffn_rows, ffn_pull = jax.vjp(token_mix, normed_ffn, ffn_edge, coefs[6:])
    ffn_mix = ffn_rows[0].reshape(rows, width).astype(BF)
    ffn_hidden = project(ffn_mix, ffn_key)
    ffn_act = jnp.square(jax.nn.relu(ffn_hidden)).astype(BF)
    ffn_result = project(ffn_act, ffn_value).reshape(inputs.shape)
    output = (valid_mask * (resid + ffn_result)).astype(BF)

    grad_out = valid_mask * cotangent.astype(jnp.float32)
    grad_ffn = grad_out.reshape(rows, width).astype(BF)
    grad_ffn_value = weight_backward(ffn_act, grad_ffn)
    grad_hidden = (
        input_backward(grad_ffn, ffn_value) * 2.0 * jax.nn.relu(ffn_hidden)
    ).astype(BF)
    grad_ffn_key = weight_backward(ffn_mix, grad_hidden)
    key_sum = scatter_rows(grad_ffn_key.astype(BF).reshape(devices, own, -1))
    value_sum = scatter_rows(
        grad_ffn_value.astype(BF).reshape(devices, feedforward_value.shape[0], width)
    )
    grad_ffn_mix = input_backward(grad_hidden, ffn_key).reshape(inputs.shape)
    grad_normed_ffn, grad_ffn_edge, grad_coef_ffn = ffn_pull((grad_ffn_mix,))
    returned_ffn = shifted(grad_ffn_edge, "seq", -1)
    grad_normed_ffn = grad_normed_ffn.at[:, -1:].add(returned_ffn)
    grad_resid, grad_gain_ffn, grad_bias_ffn = norm_ffn_pull(grad_normed_ffn)
    grad_resid = grad_resid + grad_out
    grad_attn = grad_resid.reshape(rows, width).astype(BF)
    grad_out_weight = weight_backward(attn_in, grad_attn)
    grad_attn_pre = input_backward(grad_attn, weight_o)
    (
        grad_wkv,
        direct_recep,
        direct_keys,
        direct_values,
        grad_gate_value,
        grad_own,
        grad_group_gain,
        grad_group_bias,
    ) = combine_pull(grad_attn_pre)
    grad_state = scan_states(transfer, back_offset(grad_wkv, q0), -1)
    back_recep, back_keys, back_values, back_unit, back_rate, back_decay = rec_backward(
        *streams, inverse, w0, uv, grad_wkv, state_in, grad_state
    )
    grad_keys_raw, grad_dl, grad_rl, grad_decay_base, grad_rate_base, grad_key_scales = prep_pull(
        (back_decay, back_keys + direct_keys, back_unit, back_rate)
    )
    low_recep = (back_recep + direct_recep).astype(BF)
    low_keys = grad_keys_raw.astype(BF)
    low_values = (back_values + direct_values).astype(BF)
    grad_mix = [
        weight_backward(recep_mix, low_recep),
        weight_backward(key_mix, low_keys),
        weight_backward(value_mix, low_values),
    ]
    grad_recep_mix = input_backward(low_recep, weight_r)
    grad_key_mix = input_backward(low_keys, weight_k)
    grad_value_mix = input_backward(low_values, weight_v)
    low_dl = grad_dl.astype(BF)
    grad_decay_up = weight_backward(decay_hidden, low_dl)
    low_dh = (input_backward(low_dl, up[:cut0]) * (1.0 - decay_tanh * decay_tanh)).astype(BF)
    grad_decay_down = weight_backward(decay_mix, low_dh)
    grad_decay_mix = input_backward(low_dh, down[:, :cut0])
    low_rl = grad_rl.astype(BF)
    grad_rate_up = weight_backward(rate_hidden, low_rl)
    low_rh = input_backward(low_rl, up[cut0:cut1]).astype(BF)
    grad_rate_down = weight_backward(rate_mix, low_rh)
    grad_rate_mix = input_backward(low_rh, down[:, cut0:cut1])
    low_gv = grad_gate_value.astype(BF)
    grad_gate_up = weight_backward(gate_low, low_gv)
    low_gh = (input_backward(low_gv, up[cut1:]) * gate_sig * (1.0 - gate_sig)).astype(BF)
    grad_gate_down = weight_backward(gate_mix, low_gh)
    grad_gate_mix = input_backward(low_gh, down[:, cut1:])
    grad_mixed = tuple(
        item.reshape(inputs.shape)
        for item in (
            grad_recep_mix,
            grad_decay_mix,
            grad_key_mix,
            grad_value_mix,
            grad_rate_mix,
            grad_gate_mix,
        )
    )
    grad_normed, grad_left_edge, grad_coef_mix = mix_pull(grad_mixed)
    returned_mix = shifted(grad_left_edge, "seq", -1)
    grad_normed = grad_normed.at[:, -1:].add(returned_mix)
    grad_inputs, grad_gain_mix, grad_bias_mix = norm_pull(grad_normed)
    input_grad = (grad_resid + grad_inputs).astype(BF)

    def by_device(array):
        return array.astype(BF).reshape(devices, own, -1)

    grad_downs = jnp.concatenate([grad_decay_down, grad_rate_down, grad_gate_down], 1)
    grad_ups = jnp.concatenate([grad_decay_up, grad_rate_up, grad_gate_up], 0)
    grad_vecs = jnp.stack(
        [
            grad_gain_mix,
            grad_gain_ffn,
            grad_group_gain,
            grad_bias_mix,
            grad_bias_ffn,
            grad_group_bias,
            *grad_coef_mix,
            *grad_coef_ffn,
            grad_decay_base,
            grad_rate_base,
            *grad_key_scales,
            grad_own,
        ]
    )

    def by_column(array):
        return jnp.moveaxis(array.astype(BF).reshape(-1, devices, own), 1, 0).reshape(devices, -1)

    grad_small = as_rows(
        jnp.concatenate(
            [
                grad_downs.astype(BF).reshape(devices, -1),
                by_column(grad_ups),
                by_column(grad_vecs),
            ],
            1,
        ),
        width,
    )
    sums = scatter_rows(
        jnp.concatenate([by_device(item) for item in (*grad_mix, grad_out_weight)] + [grad_small], 1)
    ).astype(F32)
    mix_sum = sums[: 3 * own].reshape(3, own, width)
    out_sum = sums[3 * own : 4 * own]
    flat = sums[4 * own :].reshape(-1)
    down_sum = flat[: own * low].reshape(own, low)
    up_sum = flat[own * low : 2 * own * low].reshape(low, own)
    vec_sum = flat[2 * own * low :][: vector_count * own].reshape(vector_count, own)
    return (
        output,
        input_grad,
        mix_sum,
        out_sum,
        down_sum[:, :cut0],
        up_sum[:cut0],
        down_sum[:, cut0:cut1],
        up_sum[cut0:cut1],
        down_sum[:, cut1:],
        up_sum[cut1:],
        key_sum.astype(F32),
        value_sum.astype(F32),
        vec_sum[:3],
        vec_sum[3:6],
        jnp.concatenate([vec_sum[6:7], vec_sum[8:13]], 0),
        vec_sum[7],
        vec_sum[13],
        vec_sum[14],
        vec_sum[15:17],
        vec_sum[17],
    )


def solution(mesh):
    in_specs = (
        P("dp", "seq", None),
        P("dp"),
        P("dp", "seq", None),
        P(None, ("dp", "seq"), None),
        P(("dp", "seq"), None),
        P(("dp", "seq"), None),
        P(None, ("dp", "seq")),
        P(("dp", "seq"), None),
        P(None, ("dp", "seq")),
        P(("dp", "seq"), None),
        P(None, ("dp", "seq")),
        P(("dp", "seq"), None),
        P(("dp", "seq"), None),
        P(None, ("dp", "seq")),
        P(None, ("dp", "seq")),
        P(None, ("dp", "seq")),
        P(("dp", "seq")),
        P(("dp", "seq")),
        P(None, ("dp", "seq")),
        P(("dp", "seq")),
    )
    out_specs = (
        P("dp", "seq", None),
        P("dp", "seq", None),
        P(None, ("dp", "seq"), None),
        P(("dp", "seq"), None),
        P(("dp", "seq"), None),
        P(None, ("dp", "seq")),
        P(("dp", "seq"), None),
        P(None, ("dp", "seq")),
        P(("dp", "seq"), None),
        P(None, ("dp", "seq")),
        P(("dp", "seq"), None),
        P(("dp", "seq"), None),
        P(None, ("dp", "seq")),
        P(None, ("dp", "seq")),
        P(None, ("dp", "seq")),
        P(("dp", "seq")),
        P(("dp", "seq")),
        P(("dp", "seq")),
        P(None, ("dp", "seq")),
        P(("dp", "seq")),
    )
    return jax.shard_map(local, mesh=mesh, in_specs=in_specs, out_specs=out_specs, check_vma=False)
```

```python
from functools import partial

import jax
import jax.numpy as jnp
from jax import lax
from jax.experimental import pallas as pl
from jax.experimental.pallas import tpu as pltpu
from jax.sharding import Mesh
from jax.sharding import PartitionSpec as P

HEAD_SIZE = 64
HEADS = 16
BOTH = ("dp", "seq")

HIGH = lax.Precision.HIGHEST
LN_EPS = 1e-05
GN_EPS = 0.00064
NORM_EPS = 1e-06
F32 = jnp.float32
BF = jnp.bfloat16
PASSES = 3


def shifted(value, axis, steps):
    count = lax.axis_size(axis)
    first, last = (max(0, -steps), min(count, count - steps))
    return lax.ppermute(value, axis, [(source, source + steps) for source in range(first, last)])


def layer_norm(content_entries, gain, bias):
    center = content_entries - jnp.mean(content_entries, -1, keepdims=True)
    spread = jnp.mean(center * center, -1, keepdims=True)
    return center * lax.rsqrt(spread + LN_EPS) * gain + bias


def token_mix(standardized_entries, left_edge, coefs):
    previous = jnp.concatenate([left_edge, standardized_entries[:, :-1]], 1)
    delta = previous - standardized_entries
    return tuple(
        (standardized_entries + delta * coefs[coef_index] for coef_index in range(coefs.shape[0]))
    )


def prepare_inputs(keys_raw, decay_lora, rate_lora, decay_base, rate_base, key_scales):
    log_decay = -jnp.exp(-jax.nn.softplus(-(decay_base + decay_lora)) - 0.5)
    rate = jax.nn.sigmoid(rate_base + rate_lora)
    scaled = (keys_raw * key_scales[0]).reshape(keys_raw.shape[:-1] + (HEADS, HEAD_SIZE))
    unit = scaled * lax.rsqrt(jnp.sum(scaled * scaled, -1, keepdims=True) + NORM_EPS)
    unit = unit.reshape(keys_raw.shape)
    keys_fin = keys_raw * (1.0 + (rate - 1.0) * key_scales[1])
    return log_decay, keys_fin, unit, unit * rate


def combined_result(wkv, receptance, keys_fin, values, gate_value, own_weights, gain, bias):
    split = wkv.shape[:-1] + (HEADS, HEAD_SIZE)
    heads = wkv.reshape(split)
    center = heads - jnp.mean(heads, -1, keepdims=True)
    spread = jnp.mean(center * center, -1, keepdims=True)
    normed = (center * lax.rsqrt(spread + GN_EPS)).reshape(wkv.shape) * gain + bias
    own = jnp.sum((receptance * keys_fin * own_weights).reshape(split), -1, keepdims=True)
    return (normed + (own * values.reshape(split)).reshape(wkv.shape)) * gate_value


def dg(a,b,ca,cb):
    return lax.dot_general(a,b,(((ca,),(cb,)),((),())),preferred_element_type=F32)

def mm(a,b,ca=1,cb=0,passes=1):
    if passes==1:
        return dg(a.astype(BF),b.astype(BF),ca,cb)
    ah=a.astype(BF); bh=b.astype(BF)
    al=(a-ah.astype(F32)).astype(BF); bl=(b-bh.astype(F32)).astype(BF)
    return dg(ah,bh,ca,cb)+(dg(ah,bl,ca,cb)+dg(al,bh,ca,cb))

def iota(shape,d): return lax.broadcasted_iota(jnp.int32,shape,d)

def lanes(n):
    lane=iota((1,n),1)
    return (lane<n//2).astype(F32),(lane>=n//2).astype(F32)

def halves(x,m0,m1):
    return jnp.concatenate([x*m0,x*m1],0)

def compact(g,m0,m1):
    h=g.shape[0]//2
    return g[:h]*m0+g[h:]*m1

def scaled_inputs(r,k,kk,b,lw):
    n=lw.shape[0]
    tri=(iota((n,n),0)>=iota((n,n),1)).astype(F32)
    cum=lax.dot_general(tri,lw,(((1,),(0,)),((),())),precision=HIGH,preferred_element_type=F32)
    total=cum[n-1:n]
    center=0.5*total
    up=jnp.exp(cum-center)
    upx=jnp.exp(cum-lw-center)
    down=jnp.exp(center-cum)
    at=-kk*upx; rt=r*up; bt=b*down; kt=k*down
    return at,rt,bt,kt,center,total,up,upx,down

def score_mask(n):
    t=iota((2*n,2*n),0); s=iota((2*n,2*n),1)
    low=t<n
    tt=jnp.where(low,t,t-n); ss=jnp.where(s<n,s,s-n)
    return (ss<tt)|((ss==tt)&jnp.logical_not(low))

def invert(a,passes):
    n=a.shape[0]
    t=iota((n,n),0); s=iota((n,n),1)
    x=t^s
    inv=jnp.where(t==s,1.0,0.0)+jnp.where((x==1),a,0.0)
    b=2
    while b<n:
        off=jnp.where((x>=b)&(x<2*b),a,0.0)
        inv=inv+mm(inv,mm(off,inv,passes=passes),passes=passes)
        b*=2
    return inv

def fwd_pair(r,k,v,kk,b,lw,pt,p):
    n=r.shape[0]; m0,m1=lanes(r.shape[1])
    at,rt,bt,kt,center,total,*_=scaled_inputs(r,k,kk,b,lw)
    x=jnp.concatenate([at,rt],0); y=jnp.concatenate([bt,kt],0)
    mask=score_mask(n)
    s0=jnp.where(mask,mm(x*m0,y,1,1,p),0.0)
    s1=jnp.where(mask,mm(x*m1,y,1,1,p),0.0)
    t0=invert(s0[:n,:n],pt); t1=invert(s1[:n,:n],pt)
    vs=halves(v,m0,m1)
    akv=mm(jnp.concatenate([s0[:n,n:],s1[:n,n:]],1),vs,passes=p)
    t01=jnp.concatenate([t0,t1],1)
    w=mm(t01,halves(at,m0,m1),passes=p); uv=mm(t01,halves(akv,m0,m1),passes=p)
    rb=jnp.concatenate([s0[n:,:n],s1[n:,:n]],1); rk=jnp.concatenate([s0[n:,n:],s1[n:,n:]],1)
    q=rt+mm(rb,halves(w,m0,m1),passes=p)
    oloc=mm(rb,halves(uv,m0,m1),passes=p)+mm(rk,vs,passes=p)
    ec=jnp.exp(center); er=jnp.exp(total-center)
    q0=q*ec; w0=w*ec
    bh=bt*er; kh=kt*er
    dfull=mm(w0,bh,0,0,p); efull=mm(uv,bh,0,0,p)+mm(v,kh,0,0,p)
    half=r.shape[1]//2
    lane=iota((half,2*half),1); row=iota((half,2*half),0)
    eye=jnp.where((lane==row)|(lane==row+half),1.0,0.0)
    d=compact(dfull,m0,m1)+eye*jnp.exp(total)
    e=compact(efull,m0,m1)
    return q0,oloc,w0,uv,t01,d,e

def bwd_pair(r,k,v,kk,b,lw,t01,w0,uv,do,s_in,ds_out,p):
    n=r.shape[0]; m0,m1=lanes(r.shape[1])
    at,rt,bt,kt,center,total,up,upx,down=scaled_inputs(r,k,kk,b,lw)
    x=jnp.concatenate([at,rt],0); y=jnp.concatenate([bt,kt],0)
    mask=score_mask(n)
    s0=jnp.where(mask,mm(x*m0,y,1,1,p),0.0)
    s1=jnp.where(mask,mm(x*m1,y,1,1,p),0.0)
    ec=jnp.exp(center); er=jnp.exp(total-center)
    stil=halves(s_in*ec,m0,m1); sraw=halves(s_in,m0,m1); dst=halves(ds_out*er,m0,m1)
    u=mm(w0,sraw,1,1,p)+uv
    dos=halves(do,m0,m1)
    du=mm(jnp.concatenate([s0[n:,:n],s1[n:,:n]],0),dos,0,0,p)+mm(bt,dst,1,1,p)
    z=mm(jnp.concatenate([t01[:,:n],t01[:,n:]],0),halves(du,m0,m1),0,0,p)
    zo=jnp.concatenate([z,do],0)
    dv=mm(s0[:,n:],zo*m0,0,0,p)+mm(s1[:,n:],zo*m1,0,0,p)+mm(kt,dst,1,1,p)
    uvs=jnp.concatenate([u,v],0)
    g0=jnp.where(mask,mm(zo*m0,uvs,1,1,p),0.0)
    g1=jnp.where(mask,mm(zo*m1,uvs,1,1,p),0.0)
    dx=mm(g0,y*m0,passes=p)+mm(g1,y*m1,passes=p)+mm(zo,stil,passes=p)
    dy=mm(g0,x*m0,0,0,p)+mm(g1,x*m1,0,0,p)+mm(uvs,dst,passes=p)
    da=dx[:n]; dr=dx[n:]; db=dy[:n]; dk=dy[n:]
    if p==1:
        rnd=lambda q: q.astype(BF).astype(F32)
    else:
        rnd=lambda q:q
    gl=rnd(rt)*dr-rnd(bt)*db-rnd(kt)*dk
    ga=rnd(at)*da
    gend=jnp.sum(rnd(dst)*(stil+mm(u,bt,0,0,p)+mm(v,kt,0,0,p)),0,keepdims=True)
    tri=(iota((n,n),0)<=iota((n,n),1)).astype(F32)
    glw=lax.dot_general(tri,gl+ga,(((1,),(0,)),((),())),precision=HIGH,preferred_element_type=F32)-ga+gend
    ds=compact(mm(zo,x,0,0,p)+dst,m0,m1)*ec
    return dr*up,dk*down,dv,-da*upx,db*down,glw,ds

def fwd_kernel(pt,p,r,k,v,kk,b,lw,q0,oloc,w0,uv,t01,d,e):
    outs=fwd_pair(r[...],k[...],v[...],kk[...],b[...],lw[...],pt,p)
    for ref,val in zip((q0,oloc,w0,uv,t01,d,e),outs): ref[...]=val.astype(ref.dtype)

def bwd_kernel(p,*refs):
    outs=bwd_pair(*[q[...].astype(F32) for q in refs[:12]],p)[:6]
    for ref,val in zip(refs[12:],outs): ref[...]=val.astype(ref.dtype)


STATE = HEAD_SIZE
PAIR = 2 * HEAD_SIZE


def specs(rows):
    col = pl.BlockSpec((rows, PAIR), lambda i: (0, i))
    state = pl.BlockSpec((STATE, PAIR), lambda i: (0, i))
    wide = pl.BlockSpec((rows, 2 * rows), lambda i: (0, i))
    return col, state, wide


def rec_forward(*args):
    n, f = args[0].shape
    pairs = f // PAIR
    col, state, wide = specs(n)
    shape = jax.ShapeDtypeStruct
    return pl.pallas_call(
        partial(fwd_kernel, PASSES, PASSES),
        grid=(pairs,),
        in_specs=[col] * 6,
        out_specs=[col] * 4 + [wide, state, state],
        out_shape=[shape((n, f), F32)] * 4
        + [shape((n, pairs * 2 * n), F32)]
        + [shape((STATE, f), F32)] * 2,
        compiler_params=pltpu.CompilerParams(vmem_limit_bytes=48 << 20),
        name="rec_forward",
    )(*args)


def rec_backward(*args):
    n, f = args[0].shape
    pairs = f // PAIR
    col, state, wide = specs(n)
    return pl.pallas_call(
        partial(bwd_kernel, PASSES),
        grid=(pairs,),
        in_specs=[col] * 6 + [wide, col, col, col, state, state],
        out_specs=[col] * 6,
        out_shape=[jax.ShapeDtypeStruct((n, f), F32)] * 6,
        compiler_params=pltpu.CompilerParams(vmem_limit_bytes=48 << 20),
        name="rec_backward",
    )(*args)


def combine_kernel(side, dl_ref, el_ref, d_ref, e_ref, dn_ref, en_ref):
    m0, m1 = lanes(PAIR)
    for pair in range(d_ref.shape[1] // PAIR):
        cols = pl.ds(pair * PAIR, PAIR)
        dl = dl_ref[:, cols].astype(F32)
        el = el_ref[:, cols].astype(F32)
        d = d_ref[:, cols]
        block = halves(d, m0, m1)
        if side == 1:
            both = mm(jnp.concatenate([dl, el], 0), block, passes=PASSES)
            dn_ref[:, cols] = both[:STATE]
            en_ref[:, cols] = both[STATE:] + e_ref[:, cols]
        else:
            en_ref[:, cols] = mm(el, block, 1, 1, passes=PASSES) + e_ref[:, cols]
            right = halves(dl, m0, m1)
            dn_ref[:, cols] = mm(d, right, passes=PASSES)


def combine(side, dl, el, d, e):
    return pl.pallas_call(
        partial(combine_kernel, side),
        out_shape=[jax.ShapeDtypeStruct(d.shape, F32)] * 2,
        compiler_params=pltpu.CompilerParams(vmem_limit_bytes=32 << 20),
        name="combine_states",
    )(dl, el, d, e)


def scan_states(transfer, offset, side):
    count = lax.axis_size("seq")

    def move(value, steps):
        return shifted(value.astype(BF), "seq", side * steps)

    d, e = move(transfer, 1).astype(F32), move(offset, 1).astype(F32)
    reach = 1
    while reach < count - 1:
        d, e = combine(side, move(d, reach), move(e, reach), d, e)
        reach *= 2
    return e


def apply_state_kernel(q_ref, s_ref, o_ref, out_ref):
    m0, m1 = lanes(PAIR)
    for pair in range(q_ref.shape[1] // PAIR):
        cols = pl.ds(pair * PAIR, PAIR)
        block = halves(s_ref[:, cols], m0, m1)
        out_ref[:, cols] = o_ref[:, cols] + mm(q_ref[:, cols], block, 1, 1, passes=PASSES)


def apply_state(q, s, o):
    return pl.pallas_call(
        apply_state_kernel,
        out_shape=jax.ShapeDtypeStruct(q.shape, F32),
        compiler_params=pltpu.CompilerParams(vmem_limit_bytes=32 << 20),
        name="apply_state",
    )(q, s, o)


def back_offset_kernel(do_ref, q_ref, f_ref):
    m0, m1 = lanes(PAIR)
    for pair in range(q_ref.shape[1] // PAIR):
        cols = pl.ds(pair * PAIR, PAIR)
        f_ref[:, cols] = compact(mm(do_ref[:, cols], q_ref[:, cols], 0, 0, PASSES), m0, m1)


def back_offset(do, q):
    return pl.pallas_call(
        back_offset_kernel,
        out_shape=jax.ShapeDtypeStruct((STATE, q.shape[1]), F32),
        compiler_params=pltpu.CompilerParams(vmem_limit_bytes=32 << 20),
        name="back_offset",
    )(do, q)

def input_backward(gradient, weight):
    return lax.dot_general(
        gradient, weight, (((1,), (1,)), ((), ())), preferred_element_type=jnp.float32
    )


def weight_backward(inputs, gradient):
    return lax.dot_general(
        inputs, gradient, (((0,), (0,)), ((), ())), preferred_element_type=jnp.float32
    )


def project(inputs, weight):
    return jnp.dot(inputs, weight, preferred_element_type=jnp.float32)


def gather_rows(packed):
    return lax.all_gather(packed, BOTH, axis=0, tiled=False)


def scatter_rows(packed):
    dp, seq = lax.axis_size("dp"), lax.axis_size("seq")
    packed = packed.reshape((dp, seq) + packed.shape[1:])
    over_seq = lax.psum_scatter(packed, "seq", scatter_dimension=1, tiled=False)
    return lax.psum_scatter(over_seq, "dp", scatter_dimension=0, tiled=False)


def as_rows(flat, width):
    rows = -(-flat.shape[-1] // width)
    padding = [(0, 0)] * (flat.ndim - 1) + [(0, rows * width - flat.shape[-1])]
    return jnp.pad(flat, padding).reshape(flat.shape[:-1] + (rows, width))


def local(
    tokens,
    lengths,
    cotangent,
    attention_weights,
    output_weight,
    decay_down_matrix,
    decay_up_matrix,
    rate_down_matrix,
    rate_up_matrix,
    gate_down_matrix,
    gate_up_matrix,
    feedforward_key,
    feedforward_value,
    layer_norm_gains,
    layer_norm_biases,
    shift_coefficients,
    decay_offset_base,
    rate_logit_base,
    removal_key_scales,
    own_term_weights,
):
    slot_count, block_len, width = tokens.shape
    rows = slot_count * block_len
    own = output_weight.shape[0]
    devices = width // own
    ranks = (decay_down_matrix.shape[1], rate_down_matrix.shape[1], gate_down_matrix.shape[1])
    low = sum(ranks)
    cut0, cut1 = ranks[0], ranks[0] + ranks[1]

    downs = jnp.concatenate([decay_down_matrix, rate_down_matrix, gate_down_matrix], 1)
    ups = jnp.concatenate([decay_up_matrix, rate_up_matrix, gate_up_matrix], 0)
    vectors = jnp.concatenate(
        [
            layer_norm_gains,
            layer_norm_biases,
            shift_coefficients,
            decay_offset_base[None],
            rate_logit_base[None],
            removal_key_scales,
            own_term_weights[None],
        ],
        0,
    )
    vector_count = vectors.shape[0]
    small = as_rows(
        jnp.concatenate([downs.reshape(-1), ups.reshape(-1), vectors.reshape(-1)]), width
    )
    packed = jnp.concatenate([attention_weights.reshape(-1, width), output_weight, small], 0)
    gathered = gather_rows(packed)
    weight_r, weight_k, weight_v, weight_o = [
        gathered[:, j * own : (j + 1) * own].reshape(width, width) for j in range(4)
    ]
    rest = gathered[:, 4 * own :].reshape(devices, -1)
    down = rest[:, : own * low].reshape(width, low)
    up = jnp.moveaxis(rest[:, own * low : 2 * own * low].reshape(devices, low, own), 0, 1)
    up = up.reshape(low, width)
    vecs = rest[:, 2 * own * low :][:, : vector_count * own].reshape(devices, vector_count, own)
    vecs = jnp.moveaxis(vecs, 0, 1).reshape(vector_count, width).astype(F32)
    gains, biases, coefs = vecs[:3], vecs[3:6], vecs[6:13]
    decay_base, rate_base, key_scales, own_weights = vecs[13], vecs[14], vecs[15:17], vecs[17]
    ffn_key = lax.all_gather(feedforward_key, BOTH, axis=0, tiled=True)
    ffn_value = lax.all_gather(feedforward_value, BOTH, axis=0, tiled=True)

    first_pos = lax.axis_index("seq") * block_len
    positions = first_pos + jnp.arange(block_len, dtype=jnp.int32)
    valid_mask = (positions[None, :] < lengths[:, None]).astype(jnp.float32)[:, :, None]
    inputs = tokens.astype(jnp.float32)
    normed, norm_pull = jax.vjp(layer_norm, inputs, gains[0], biases[0])
    left_edge = shifted(normed[:, -1:], "seq", 1)
    mixed_rows, mix_pull = jax.vjp(token_mix, normed, left_edge, coefs[:6])
    recep_mix, decay_mix, key_mix, value_mix, rate_mix, gate_mix = [
        item.reshape(rows, width).astype(BF) for item in mixed_rows
    ]
    receptance = project(recep_mix, weight_r)
    keys_raw = project(key_mix, weight_k)
    values = project(value_mix, weight_v)
    decay_tanh = jnp.tanh(project(decay_mix, down[:, :cut0]))
    decay_hidden = decay_tanh.astype(BF)
    decay_lora = project(decay_hidden, up[:cut0])
    rate_hidden = project(rate_mix, down[:, cut0:cut1]).astype(BF)
    rate_lora = project(rate_hidden, up[cut0:cut1])
    gate_sig = jax.nn.sigmoid(project(gate_mix, down[:, cut1:]))
    gate_low = gate_sig.astype(BF)
    gate_value = project(gate_low, up[cut1:])
    prepared, prep_pull = jax.vjp(
        prepare_inputs, keys_raw, decay_lora, rate_lora, decay_base, rate_base, key_scales
    )
    log_decay, keys_fin, unit, unit_rate = prepared
    streams = (receptance, keys_fin, values, unit, unit_rate, log_decay)
    q0, o_local, w0, uv, inverse, transfer, offset = rec_forward(*streams)
    state_in = scan_states(transfer, offset, 1)
    wkv = apply_state(q0, state_in, o_local)
    attn_pre, combine_pull = jax.vjp(
        combined_result,
        wkv,
        receptance,
        keys_fin,
        values,
        gate_value,
        own_weights,
        gains[2],
        biases[2],
    )
    attn_in = attn_pre.astype(BF)
    resid = inputs + project(attn_in, weight_o).reshape(inputs.shape)
    normed_ffn, norm_ffn_pull = jax.vjp(layer_norm, resid, gains[1], biases[1])
    ffn_edge = shifted(normed_ffn[:, -1:], "seq", 1)
    ffn_rows, ffn_pull = jax.vjp(token_mix, normed_ffn, ffn_edge, coefs[6:])
    ffn_mix = ffn_rows[0].reshape(rows, width).astype(BF)
    ffn_hidden = project(ffn_mix, ffn_key)
    ffn_act = jnp.square(jax.nn.relu(ffn_hidden)).astype(BF)
    ffn_result = project(ffn_act, ffn_value).reshape(inputs.shape)
    output = (valid_mask * (resid + ffn_result)).astype(BF)

    grad_out = valid_mask * cotangent.astype(jnp.float32)
    grad_ffn = grad_out.reshape(rows, width).astype(BF)
    grad_ffn_value = weight_backward(ffn_act, grad_ffn)
    grad_hidden = (
        input_backward(grad_ffn, ffn_value) * 2.0 * jax.nn.relu(ffn_hidden)
    ).astype(BF)
    grad_ffn_key = weight_backward(ffn_mix, grad_hidden)
    key_sum = scatter_rows(grad_ffn_key.astype(BF).reshape(devices, own, -1))
    value_sum = scatter_rows(
        grad_ffn_value.astype(BF).reshape(devices, feedforward_value.shape[0], width)
    )
    grad_ffn_mix = input_backward(grad_hidden, ffn_key).reshape(inputs.shape)
    grad_normed_ffn, grad_ffn_edge, grad_coef_ffn = ffn_pull((grad_ffn_mix,))
    returned_ffn = shifted(grad_ffn_edge, "seq", -1)
    grad_normed_ffn = grad_normed_ffn.at[:, -1:].add(returned_ffn)
    grad_resid, grad_gain_ffn, grad_bias_ffn = norm_ffn_pull(grad_normed_ffn)
    grad_resid = grad_resid + grad_out
    grad_attn = grad_resid.reshape(rows, width).astype(BF)
    grad_out_weight = weight_backward(attn_in, grad_attn)
    grad_attn_pre = input_backward(grad_attn, weight_o)
    (
        grad_wkv,
        direct_recep,
        direct_keys,
        direct_values,
        grad_gate_value,
        grad_own,
        grad_group_gain,
        grad_group_bias,
    ) = combine_pull(grad_attn_pre)
    grad_state = scan_states(transfer, back_offset(grad_wkv, q0), -1)
    back_recep, back_keys, back_values, back_unit, back_rate, back_decay = rec_backward(
        *streams, inverse, w0, uv, grad_wkv, state_in, grad_state
    )
    grad_keys_raw, grad_dl, grad_rl, grad_decay_base, grad_rate_base, grad_key_scales = prep_pull(
        (back_decay, back_keys + direct_keys, back_unit, back_rate)
    )
    low_recep = (back_recep + direct_recep).astype(BF)
    low_keys = grad_keys_raw.astype(BF)
    low_values = (back_values + direct_values).astype(BF)
    grad_mix = [
        weight_backward(recep_mix, low_recep),
        weight_backward(key_mix, low_keys),
        weight_backward(value_mix, low_values),
    ]
    grad_recep_mix = input_backward(low_recep, weight_r)
    grad_key_mix = input_backward(low_keys, weight_k)
    grad_value_mix = input_backward(low_values, weight_v)
    low_dl = grad_dl.astype(BF)
    grad_decay_up = weight_backward(decay_hidden, low_dl)
    low_dh = (input_backward(low_dl, up[:cut0]) * (1.0 - decay_tanh * decay_tanh)).astype(BF)
    grad_decay_down = weight_backward(decay_mix, low_dh)
    grad_decay_mix = input_backward(low_dh, down[:, :cut0])
    low_rl = grad_rl.astype(BF)
    grad_rate_up = weight_backward(rate_hidden, low_rl)
    low_rh = input_backward(low_rl, up[cut0:cut1]).astype(BF)
    grad_rate_down = weight_backward(rate_mix, low_rh)
    grad_rate_mix = input_backward(low_rh, down[:, cut0:cut1])
    low_gv = grad_gate_value.astype(BF)
    grad_gate_up = weight_backward(gate_low, low_gv)
    low_gh = (input_backward(low_gv, up[cut1:]) * gate_sig * (1.0 - gate_sig)).astype(BF)
    grad_gate_down = weight_backward(gate_mix, low_gh)
    grad_gate_mix = input_backward(low_gh, down[:, cut1:])
    grad_mixed = tuple(
        item.reshape(inputs.shape)
        for item in (
            grad_recep_mix,
            grad_decay_mix,
            grad_key_mix,
            grad_value_mix,
            grad_rate_mix,
            grad_gate_mix,
        )
    )
    grad_normed, grad_left_edge, grad_coef_mix = mix_pull(grad_mixed)
    returned_mix = shifted(grad_left_edge, "seq", -1)
    grad_normed = grad_normed.at[:, -1:].add(returned_mix)
    grad_inputs, grad_gain_mix, grad_bias_mix = norm_pull(grad_normed)
    input_grad = (grad_resid + grad_inputs).astype(BF)

    def by_device(array):
        return array.astype(BF).reshape(devices, own, -1)

    grad_downs = jnp.concatenate([grad_decay_down, grad_rate_down, grad_gate_down], 1)
    grad_ups = jnp.concatenate([grad_decay_up, grad_rate_up, grad_gate_up], 0)
    grad_vecs = jnp.stack(
        [
            grad_gain_mix,
            grad_gain_ffn,
            grad_group_gain,
            grad_bias_mix,
            grad_bias_ffn,
            grad_group_bias,
            *grad_coef_mix,
            *grad_coef_ffn,
            grad_decay_base,
            grad_rate_base,
            *grad_key_scales,
            grad_own,
        ]
    )

    def by_column(array):
        return jnp.moveaxis(array.astype(BF).reshape(-1, devices, own), 1, 0).reshape(devices, -1)

    grad_small = as_rows(
        jnp.concatenate(
            [
                grad_downs.astype(BF).reshape(devices, -1),
                by_column(grad_ups),
                by_column(grad_vecs),
            ],
            1,
        ),
        width,
    )
    sums = scatter_rows(
        jnp.concatenate([by_device(item) for item in (*grad_mix, grad_out_weight)] + [grad_small], 1)
    ).astype(F32)
    mix_sum = sums[: 3 * own].reshape(3, own, width)
    out_sum = sums[3 * own : 4 * own]
    flat = sums[4 * own :].reshape(-1)
    down_sum = flat[: own * low].reshape(own, low)
    up_sum = flat[own * low : 2 * own * low].reshape(low, own)
    vec_sum = flat[2 * own * low :][: vector_count * own].reshape(vector_count, own)
    return (
        output,
        input_grad,
        mix_sum,
        out_sum,
        down_sum[:, :cut0],
        up_sum[:cut0],
        down_sum[:, cut0:cut1],
        up_sum[cut0:cut1],
        down_sum[:, cut1:],
        up_sum[cut1:],
        key_sum.astype(F32),
        value_sum.astype(F32),
        vec_sum[:3],
        vec_sum[3:6],
        jnp.concatenate([vec_sum[6:7], vec_sum[8:13]], 0),
        vec_sum[7],
        vec_sum[13],
        vec_sum[14],
        vec_sum[15:17],
        vec_sum[17],
    )


SEQ = ("chip", "core")
ALL = ("dp", "chip", "core")
LANES = 128
E_HALF = 1.6487212707001282


def params(limit=56):
    return pltpu.CompilerParams(
        dimension_semantics=("arbitrary",), vmem_limit_bytes=limit << 20
    )


def cost(us):
    return pl.CostEstimate(flops=us * 10**9, bytes_accessed=us * 10**6, transcendentals=0)


def whole(shape):
    return pl.BlockSpec(shape, lambda i: (0,) * len(shape))


def nt(a, b):
    return dg(a.astype(BF), b.astype(BF), 1, 1)


def nn(a, b):
    return dg(a.astype(BF), b.astype(BF), 1, 0)


def tn(a, b):
    return dg(a.astype(BF), b.astype(BF), 0, 0)


def head_sum(x, m0, m1):
    s0 = jnp.sum(x * m0, -1, keepdims=True)
    s1 = jnp.sum(x * m1, -1, keepdims=True)
    return s0 * m0 + s1 * m1


def norm_parts(x):
    center = x - jnp.mean(x, -1, keepdims=True)
    rstd = lax.rsqrt(jnp.mean(center * center, -1, keepdims=True) + LN_EPS)
    return center * rstd, rstd


def shift_down(x, first):
    rolled = pltpu.roll(x, 1, 0)
    return jnp.where(iota(x.shape, 0) == 0, first, rolled)


def shift_up(x):
    n = x.shape[0]
    rolled = pltpu.roll(x, n - 1, 0)
    return jnp.where(iota(x.shape, 0) == n - 1, 0.0, rolled)


def mixes(normed, delta, vec_ref):
    return [(normed + delta * vec_ref[6 + j : 7 + j]).astype(BF) for j in range(6)]


def low_act(h, m0):
    return jnp.where(m0 > 0, jnp.tanh(h), h)


def project_kernel(x_ref, w_ref, down_ref, up_ref, vec_ref, own_ref, *rest):
    r_ref, k_ref, v_ref, lw_ref, rate_ref, gv_ref, h_ref, carry = rest
    width = x_ref.shape[1]
    m0, m1 = lanes(LANES)

    @pl.when(pl.program_id(0) == 0)
    def _():
        carry[...] = jnp.zeros_like(carry)

    unit, _ = norm_parts(x_ref[...].astype(F32))
    normed = unit * vec_ref[0:1] + vec_ref[3:4]
    delta = shift_down(normed, carry[0:1]) - normed
    carry[...] = jnp.broadcast_to(normed[-1:], carry.shape)
    m_r, m_w, m_k, m_v, m_a, m_g = mixes(normed, delta, vec_ref)
    weights = [w_ref[:, j].reshape(width, LANES) for j in range(3)]
    r_ref[...] = nn(m_r, weights[0])
    k_ref[...] = nn(m_k, weights[1])
    v_ref[...] = nn(m_v, weights[2])
    down0 = down_ref[:, :LANES]
    h_low = jnp.where(m0 > 0, nn(m_w, down0), nn(m_a, down0))
    h_gate = nn(m_g, down_ref[:, LANES:])
    h_ref[:, :LANES] = h_low
    h_ref[:, LANES:] = h_gate
    act = low_act(h_low, m0).astype(BF).astype(F32)
    dl = nt(act * m0, up_ref[:, :LANES])
    rl = nt(act * m1, up_ref[:, :LANES])
    gv_ref[...] = nt(jax.nn.sigmoid(h_gate), up_ref[:, LANES:])
    lw_ref[...] = jax.nn.sigmoid(own_ref[0:1] + dl) * (-1.0 / E_HALF)
    rate_ref[...] = jax.nn.sigmoid(own_ref[1:2] + rl)


def project_call(x, w, down, up, vec, own):
    n, width = x.shape
    rows = w.shape[0] and LANES
    block = pl.BlockSpec((rows, LANES), lambda i: (i, 0))
    return pl.pallas_call(
        project_kernel,
        grid=(n // rows,),
        in_specs=[pl.BlockSpec((rows, width), lambda i: (i, 0))]
        + [whole(a.shape) for a in (w, down, up, vec, own)],
        out_specs=[block] * 6 + [pl.BlockSpec((rows, 2 * LANES), lambda i: (i, 0))],
        out_shape=[jax.ShapeDtypeStruct((n, LANES), F32)] * 6
        + [jax.ShapeDtypeStruct((n, 2 * LANES), F32)],
        scratch_shapes=[pltpu.VMEM((8, width), F32)],
        compiler_params=params(),
        cost_estimate=cost(10),
        name="project",
    )(x, w, down, up, vec, own)


def key_parts(kraw, rate, own_ref, m0, m1):
    scaled = kraw * own_ref[2:3]
    rs = lax.rsqrt(head_sum(scaled * scaled, m0, m1) + NORM_EPS)
    unit = scaled * rs
    keys = kraw * (1.0 + (rate - 1.0) * own_ref[3:4])
    return unit, rs, keys


def group_norm(wkv, m0, m1):
    center = wkv - head_sum(wkv, m0, m1) * (1.0 / HEAD_SIZE)
    spread = head_sum(center * center, m0, m1) * (1.0 / HEAD_SIZE)
    rstd = lax.rsqrt(spread + GN_EPS)
    return center * rstd, rstd


def recur_kernel(r_ref, k_ref, v_ref, lw_ref, rate_ref, gv_ref, own_ref, *rest):
    attn_ref, wkv_ref, w0_ref, uv_ref, inv_ref, st_ref, state = rest
    m0, m1 = lanes(LANES)

    @pl.when(pl.program_id(0) == 0)
    def _():
        state[...] = jnp.zeros_like(state)

    r, v, rate = r_ref[...], v_ref[...], rate_ref[...]
    unit, _, keys = key_parts(k_ref[...], rate, own_ref, m0, m1)
    q0, oloc, w0, uv, t01, d, e = fwd_pair(
        r, keys, v, unit, unit * rate, lw_ref[...], PASSES, PASSES
    )
    s = state[...]
    st_ref[...] = s
    wkv = oloc + mm(q0, halves(s, m0, m1), 1, 1, PASSES)
    state[...] = mm(s, halves(d, m0, m1), passes=PASSES) + e
    normed, _ = group_norm(wkv, m0, m1)
    bonus = head_sum(r * keys * own_ref[4:5], m0, m1)
    pre = normed * own_ref[5:6] + own_ref[6:7] + bonus * v
    attn_ref[...] = (pre * gv_ref[...]).astype(BF)
    wkv_ref[...] = wkv
    w0_ref[...] = w0
    uv_ref[...] = uv
    inv_ref[...] = t01


def recur_call(r, k, v, lw, rate, gv, own):
    n = r.shape[0]
    c = LANES
    block = pl.BlockSpec((c, LANES), lambda i: (i, 0))
    shape = jax.ShapeDtypeStruct
    return pl.pallas_call(
        recur_kernel,
        grid=(n // c,),
        in_specs=[block] * 6 + [whole(own.shape)],
        out_specs=[block] * 4
        + [
            pl.BlockSpec((c, 2 * c), lambda i: (i, 0)),
            pl.BlockSpec((STATE, LANES), lambda i: (i, 0)),
        ],
        out_shape=[shape((n, LANES), BF)]
        + [shape((n, LANES), F32)] * 3
        + [shape((n, 2 * c), F32), shape((n // c * STATE, LANES), F32)],
        scratch_shapes=[pltpu.VMEM((STATE, LANES), F32)],
        compiler_params=params(),
        cost_estimate=cost(40),
        name="recur",
    )(r, k, v, lw, rate, gv, own)


def ffn_kernel(
    where_ref, x_ref, mine_ref, other_ref, cot_ref, wo_in_ref, kv_ref, vec_ref, *rest
):
    part_ref, back_ref, resid_ref, gkv_ref, *rest = rest
    carry, wo_ref, key_ref, acc_key, acc_value = rest
    step = pl.program_id(0)
    rows, width = x_ref.shape
    ff = kv_ref.shape[0]
    value_ref = kv_ref.at[:, width:]
    core = where_ref[2]

    @pl.when(step == 0)
    def _():
        for q in range(mine_ref.shape[0]):
            for c in range(2):
                at = pl.multiple_of((2 * q + (c + core) % 2) * LANES, LANES)
                wo_ref[(2 * q + c) * LANES : (2 * q + c + 1) * LANES] = wo_in_ref[
                    pl.ds(at, LANES)
                ]
        for part in range(width // LANES):
            key_ref[part * LANES : (part + 1) * LANES] = kv_ref[
                part // 2 * LANES : (part // 2 + 1) * LANES, part % 2 * ff : (part % 2 + 1) * ff
            ]
        carry[...] = jnp.zeros_like(carry)
        acc_key[...] = jnp.zeros_like(acc_key)
        acc_value[...] = jnp.zeros_like(acc_value)

    attn = jnp.concatenate(
        [ref[q] for q in range(mine_ref.shape[0]) for ref in (mine_ref, other_ref)], 1
    )
    resid = x_ref[...].astype(F32) + nn(attn, wo_ref[...])

    @pl.when(step == where_ref[0])
    def _():
        resid_ref[0:rows] = resid

    @pl.when(step == where_ref[0] - 1)
    def _():
        resid_ref[rows : 2 * rows] = resid

    unit, _ = norm_parts(resid)
    normed = unit * vec_ref[1:2] + vec_ref[4:5]
    mix = (normed + (shift_down(normed, carry[0:1]) - normed) * vec_ref[12:13]).astype(BF)
    carry[...] = jnp.broadcast_to(normed[-1:], carry.shape)
    relu = jnp.maximum(nn(mix, key_ref[...]), 0.0)
    act = (relu * relu).astype(BF)
    part_ref[...] = nn(act, value_ref[...]).astype(BF)
    position = step * rows + iota((rows, 1), 0)
    g_ffn = jnp.where(position < where_ref[1], cot_ref[...], jnp.zeros((), BF))
    acc_value[...] += tn(act, g_ffn)
    g_hidden = (nt(g_ffn, value_ref[...]) * 2.0 * relu).astype(BF)
    acc_key[...] += tn(mix, g_hidden)
    g_mix = nt(g_hidden, key_ref[...]).astype(BF)
    back_ref[step, 0:rows] = g_mix
    back_ref[step, rows:] = jnp.zeros((back_ref.shape[1] - rows, width), BF)

    @pl.when(step > 0)
    def _():
        back_ref[jnp.maximum(step - 1, 0), rows:] = g_mix[: back_ref.shape[1] - rows]

    @pl.when(step == pl.num_programs(0) - 1)
    def _():
        gkv_ref[:, width:] = acc_value[...].astype(BF)
        for part in range(width // LANES):
            gkv_ref[
                part // 2 * LANES : (part // 2 + 1) * LANES, part % 2 * ff : (part % 2 + 1) * ff
            ] = acc_key[part * LANES : (part + 1) * LANES].astype(BF)


EDGE = 16


def ffn_call(where, x, mine, other, cot, wo, kv, vec):
    n, width = x.shape
    ff = kv.shape[0]
    rows = LANES
    blocks = n // rows
    shape = jax.ShapeDtypeStruct
    row = pl.BlockSpec((rows, width), lambda i: (i, 0))
    heads = pl.BlockSpec((mine.shape[0], rows, LANES), lambda i: (0, i, 0))
    return pl.pallas_call(
        ffn_kernel,
        grid=(blocks,),
        in_specs=[pl.BlockSpec(memory_space=pltpu.SMEM), row, heads, heads, row]
        + [whole(a.shape) for a in (wo, kv, vec)],
        out_specs=[
            row,
            whole((blocks, rows + EDGE, width)),
            whole((2 * rows, width)),
            whole(kv.shape),
        ],
        out_shape=[
            shape((n, width), BF),
            shape((blocks, rows + EDGE, width), BF),
            shape((2 * rows, width), F32),
            shape(kv.shape, BF),
        ],
        scratch_shapes=[
            pltpu.VMEM((8, width), F32),
            pltpu.VMEM((width, width), BF),
            pltpu.VMEM((width, ff), BF),
            pltpu.VMEM((width, ff), F32),
            pltpu.VMEM((ff, width), F32),
        ],
        compiler_params=params(),
        cost_estimate=cost(25),
        name="ffn",
    )(where, x, mine, other, cot, wo, kv, vec)


def norm_back(q, unit, rstd):
    return rstd * (
        q
        - jnp.mean(q, -1, keepdims=True)
        - unit * jnp.mean(q * unit, -1, keepdims=True)
    )


def add_next(grad, coef, edge):
    kept = shift_up(grad)
    last = iota(grad.shape, 0) == grad.shape[0] - 1
    return grad * (1.0 - coef) + jnp.where(last, edge, kept) * coef


def resid_kernel(
    where_ref, back_ref, resid_ref, cot_ref, mine_ref, other_ref, wo_ref, vec_ref, *rest
):
    gres_ref, gin_ref, gwo_ref, sums_ref = rest
    rows = cot_ref.shape[0]
    width = cot_ref.shape[1]
    total = jnp.sum(back_ref[...].astype(F32), 0)
    grad = total[:rows]
    position = where_ref[0] * rows + iota((rows, 1), 0)
    g_out = jnp.where(position < where_ref[1], cot_ref[...].astype(F32), 0.0)
    coef = vec_ref[12:13]
    unit, rstd = norm_parts(resid_ref[0:rows])
    normed = unit * vec_ref[1:2] + vec_ref[4:5]
    before, _ = norm_parts(resid_ref[2 * rows - 8 :])
    before = before * vec_ref[1:2] + vec_ref[4:5]
    first = jnp.where(where_ref[0] > 0, before[7:8], 0.0)
    prev = shift_down(normed, first)
    g_coef = jnp.sum((prev - normed) * grad, 0, keepdims=True)
    g_normed = add_next(grad, coef, total[rows : rows + 1])
    g_gain = jnp.sum(g_normed * unit, 0, keepdims=True)
    g_bias = jnp.sum(g_normed, 0, keepdims=True)
    g_resid = g_out + norm_back(g_normed * vec_ref[1:2], unit, rstd)
    gres_ref[...] = g_resid
    g_attn = g_resid.astype(BF)
    g_in = nt(g_attn, wo_ref[...]).astype(BF)
    for s in range(gin_ref.shape[0]):
        gin_ref[s] = g_in[:, s * LANES : (s + 1) * LANES]
    core = where_ref[2]
    for q in range(mine_ref.shape[0]):
        for c, ref in enumerate((mine_ref, other_ref)):
            at = pl.multiple_of((2 * q + (c + core) % 2) * LANES, LANES)
            gwo_ref[pl.ds(at, LANES)] = tn(ref[q], g_attn).astype(BF)
    sums_ref[...] = jnp.concatenate(
        [g_gain, g_bias, g_coef, jnp.zeros((5, width), F32)], 0
    )


def resid_call(where, back, resid, cot, mine, other, wo, vec):
    rows, width = cot.shape
    shape = jax.ShapeDtypeStruct
    seq = 2 * mine.shape[0]
    vm = pl.BlockSpec(memory_space=pltpu.VMEM)
    return pl.pallas_call(
        resid_kernel,
        in_specs=[pl.BlockSpec(memory_space=pltpu.SMEM)] + [vm] * 7,
        out_specs=[vm] * 4,
        out_shape=[
            shape((rows, width), F32),
            shape((seq, rows, LANES), BF),
            shape((width, width), BF),
            shape((8, width), F32),
        ],
        compiler_params=pltpu.CompilerParams(vmem_limit_bytes=56 << 20),
        cost_estimate=cost(6),
        name="resid_back",
    )(where, back, resid, cot, mine, other, wo, vec)


def recur_back_kernel(
    r_ref, k_ref, v_ref, lw_ref, rate_ref, gv_ref, own_ref, wkv_ref, w0_ref, uv_ref, *rest
):
    inv_ref, st_ref, gin_ref, g_ref, sums_ref, dstate, acc = rest
    m0, m1 = lanes(LANES)

    @pl.when(pl.program_id(0) == 0)
    def _():
        dstate[...] = jnp.zeros_like(dstate)
        acc[...] = jnp.zeros_like(acc)

    r, kraw, v, rate, gv = r_ref[...], k_ref[...], v_ref[...], rate_ref[...], gv_ref[...]
    lw = lw_ref[...]
    unit, rs, keys = key_parts(kraw, rate, own_ref, m0, m1)
    gain, bias, own_w = own_ref[5:6], own_ref[6:7], own_ref[4:5]
    normed, rstd = group_norm(wkv_ref[...], m0, m1)
    bonus = head_sum(r * keys * own_w, m0, m1)
    g_in = gin_ref[...].astype(F32)
    g_gv = g_in * (normed * gain + bias + bonus * v)
    g_pre = g_in * gv
    g_norm = g_pre * gain
    mean = 1.0 / HEAD_SIZE
    d_out = rstd * (
        g_norm
        - head_sum(g_norm, m0, m1) * mean
        - normed * (head_sum(g_norm * normed, m0, m1) * mean)
    )
    g_bonus = head_sum(g_pre * v, m0, m1)
    dr, dk, dv, dkk, db, glw, ds = bwd_pair(
        r,
        keys,
        v,
        unit,
        unit * rate,
        lw,
        inv_ref[...],
        w0_ref[...],
        uv_ref[...],
        d_out,
        st_ref[...],
        dstate[...],
        PASSES,
    )
    dstate[...] = ds
    dr = dr + g_bonus * keys * own_w
    dv = dv + g_pre * bonus
    dk = dk + g_bonus * r * own_w
    ks1 = own_ref[3:4]
    g_unit = dkk + db * rate
    g_rate = db * unit + dk * kraw * ks1
    g_scaled = rs * (g_unit - unit * head_sum(g_unit * unit, m0, m1))
    g_kraw = dk * (1.0 + (rate - 1.0) * ks1) + g_scaled * own_ref[2:3]
    g_rl = g_rate * rate * (1.0 - rate)
    g_dl = glw * lw * (1.0 + lw * E_HALF)
    for j, item in enumerate((dr, g_kraw, dv, g_dl, g_rl, g_gv)):
        g_ref[:, j * LANES : (j + 1) * LANES] = item.astype(BF)
    rows = [
        g_dl,
        g_rl,
        g_scaled * kraw,
        dk * kraw * (rate - 1.0),
        g_bonus * r * keys,
        g_pre * normed,
        g_pre,
    ]
    sums = [jnp.sum(item, 0, keepdims=True) for item in rows] + [jnp.zeros((1, LANES), F32)]
    acc[...] += jnp.concatenate(sums, 0)
    sums_ref[...] = acc[...]


def recur_back_call(r, k, v, lw, rate, gv, own, wkv, w0, uv, inverse, states, gin):
    n = r.shape[0]
    c = LANES
    last = n // c - 1
    block = pl.BlockSpec((c, LANES), lambda i: (last - i, 0))
    shape = jax.ShapeDtypeStruct
    return pl.pallas_call(
        recur_back_kernel,
        grid=(n // c,),
        in_specs=[block] * 6
        + [whole(own.shape)]
        + [block] * 3
        + [
            pl.BlockSpec((c, 2 * c), lambda i: (last - i, 0)),
            pl.BlockSpec((STATE, LANES), lambda i: (last - i, 0)),
            block,
        ],
        out_specs=[
            pl.BlockSpec((c, 6 * LANES), lambda i: (last - i, 0)),
            whole((8, LANES)),
        ],
        out_shape=[shape((n, 6 * LANES), BF), shape((8, LANES), F32)],
        scratch_shapes=[pltpu.VMEM((STATE, LANES), F32), pltpu.VMEM((8, LANES), F32)],
        compiler_params=params(),
        cost_estimate=cost(23),
        name="recur_back",
    )(r, k, v, lw, rate, gv, own, wkv, w0, uv, inverse, states, gin)


def project_back_kernel(x_ref, g_ref, h_ref, w_ref, down_ref, up_ref, vec_ref, *rest):
    back_ref, gw_ref, gdown_ref, gup_ref, coef_ref, carry, acc_w, acc_down, acc_up, acc_c = rest
    step = pl.program_id(0)
    rows, width = x_ref.shape
    m0, m1 = lanes(LANES)

    @pl.when(step == 0)
    def _():
        for item in (carry, acc_w, acc_down, acc_up, acc_c):
            item[...] = jnp.zeros_like(item)

    unit, _ = norm_parts(x_ref[...].astype(F32))
    normed = unit * vec_ref[0:1] + vec_ref[3:4]
    before = shift_down(unit, carry[0:1])
    seen = jnp.where(step * rows + iota((rows, 1), 0) > 0, 1.0, 0.0)
    delta = (before * vec_ref[0:1] + vec_ref[3:4]) * seen - normed
    carry[...] = jnp.broadcast_to(unit[-1:], carry.shape)
    m_r, m_w, m_k, m_v, m_a, m_g = mixes(normed, delta, vec_ref)
    g_r, g_k, g_v, g_dl, g_rl, g_gv = [
        g_ref[:, j * LANES : (j + 1) * LANES] for j in range(6)
    ]
    for j, (m, g) in enumerate(((m_r, g_r), (m_k, g_k), (m_v, g_v))):
        acc_w[j] += tn(m, g)
    h_low = h_ref[:, :LANES]
    act = low_act(h_low, m0)
    sig = jax.nn.sigmoid(h_ref[:, LANES:])
    up0, up1 = up_ref[:, :LANES], up_ref[:, LANES:]
    back_low = jnp.where(m0 > 0, nn(g_dl, up0) * (1.0 - act * act), nn(g_rl, up0))
    low_w = (back_low * m0).astype(BF)
    low_a = (back_low * m1).astype(BF)
    low_g = (nn(g_gv, up1) * sig * (1.0 - sig)).astype(BF)
    rounded = act.astype(BF).astype(F32)
    acc_up[:, :LANES] += tn(g_dl, rounded * m0) + tn(g_rl, rounded * m1)
    acc_up[:, LANES:] += tn(g_gv, sig)
    acc_down[:, :LANES] += tn(m_w, low_w) + tn(m_a, low_a)
    acc_down[:, LANES:] += tn(m_g, low_g)
    down0, down1 = down_ref[:, :LANES], down_ref[:, LANES:]
    weights = [w_ref[:, j].reshape(width, LANES) for j in range(3)]
    here = jnp.zeros((rows, width), F32)
    later = jnp.zeros((rows, width), F32)
    branches = (
        (g_r, weights[0]),
        (low_w, down0),
        (g_k, weights[1]),
        (g_v, weights[2]),
        (low_a, down0),
        (low_g, down1),
    )
    for j, (g, w) in enumerate(branches):
        g_m = nt(g, w)
        later_j = g_m * vec_ref[6 + j : 7 + j]
        here = here + (g_m - later_j)
        later = later + later_j
        acc_c[j : j + 1] += jnp.sum(delta * g_m, 0, keepdims=True)
    acc_c[6:7] += jnp.sum(here * unit + later * (before * seen), 0, keepdims=True)
    acc_c[7:8] += jnp.sum(here + later * seen, 0, keepdims=True)
    back_ref[step, 0:rows] = (here + shift_up(later)).astype(BF)
    back_ref[step, rows:] = jnp.zeros((EDGE, width), BF)

    @pl.when(step > 0)
    def _():
        back_ref[jnp.maximum(step - 1, 0), rows:] = later[:EDGE].astype(BF)

    @pl.when(step == pl.num_programs(0) - 1)
    def _():
        shape = (gw_ref.shape[0], gw_ref.shape[2], LANES)
        for j in range(3):
            gw_ref[:, j] = acc_w[j].astype(BF).reshape(shape)
        gdown_ref[...] = acc_down[...].astype(BF)
        gup_ref[...] = acc_up[...].astype(BF)
        coef_ref[...] = acc_c[...]


def project_back_call(x, g, h, w, down, up, vec):
    n, width = x.shape
    rows = LANES
    blocks = n // rows
    shape = jax.ShapeDtypeStruct
    return pl.pallas_call(
        project_back_kernel,
        grid=(blocks,),
        in_specs=[
            pl.BlockSpec((rows, width), lambda i: (i, 0)),
            pl.BlockSpec((rows, 6 * LANES), lambda i: (i, 0)),
            pl.BlockSpec((rows, 2 * LANES), lambda i: (i, 0)),
        ]
        + [whole(a.shape) for a in (w, down, up, vec)],
        out_specs=[
            whole((blocks, rows + EDGE, width)),
            whole(w.shape),
            whole(down.shape),
            whole(up.shape),
            whole((8, width)),
        ],
        out_shape=[
            shape((blocks, rows + EDGE, width), BF),
            shape(w.shape, BF),
            shape(down.shape, BF),
            shape(up.shape, BF),
            shape((8, width), F32),
        ],
        scratch_shapes=[
            pltpu.VMEM((8, width), F32),
            pltpu.VMEM((3, width, LANES), F32),
            pltpu.VMEM(down.shape, F32),
            pltpu.VMEM(up.shape, F32),
            pltpu.VMEM((8, width), F32),
        ],
        compiler_params=params(),
        cost_estimate=cost(19),
        name="project_back",
    )(x, g, h, w, down, up, vec)


def input_kernel(back_ref, x_ref, gres_ref, vec_ref, out_ref):
    rows = x_ref.shape[0]
    total = jnp.sum(back_ref[...].astype(F32), 0)
    grad = total[:rows]
    last = iota(grad.shape, 0) == rows - 1
    grad = grad + jnp.where(last, total[rows : rows + 1], 0.0)
    unit, rstd = norm_parts(x_ref[...].astype(F32))
    out = gres_ref[...] + norm_back(grad * vec_ref[0:1], unit, rstd)
    out_ref[...] = out.astype(BF)


def input_call(back, x, gres, vec):
    vm = pl.BlockSpec(memory_space=pltpu.VMEM)
    return pl.pallas_call(
        input_kernel,
        in_specs=[vm] * 4,
        out_specs=vm,
        out_shape=jax.ShapeDtypeStruct(x.shape, BF),
        compiler_params=pltpu.CompilerParams(vmem_limit_bytes=56 << 20),
        cost_estimate=cost(3),
        name="input_back",
    )(back, x, gres, vec)


def exchange(x, axis):
    return lax.all_to_all(x, axis, 0, 0, tiled=True)


def swap_cores(x):
    return lax.ppermute(x, "core", [(0, 1), (1, 0)])


def spread(x):
    chips = lax.axis_size("chip")
    mine = exchange(jnp.broadcast_to(x[None], (chips,) + x.shape), "chip")
    return mine, swap_cores(mine)


def collect(x):
    chips = lax.axis_size("chip")
    split = x.reshape((chips, 2) + x.shape[1:])
    core = lax.axis_index("core")
    keep = lax.dynamic_index_in_dim(split, core, 1, False)
    give = lax.dynamic_index_in_dim(split, 1 - core, 1, False)
    part = (keep.astype(F32) + swap_cores(give).astype(F32)).astype(BF)
    return exchange(part, "chip")


def local_slot(
    tokens,
    lengths,
    cotangent,
    attention_weights,
    output_weight,
    decay_down_matrix,
    decay_up_matrix,
    rate_down_matrix,
    rate_up_matrix,
    gate_down_matrix,
    gate_up_matrix,
    feedforward_key,
    feedforward_value,
    layer_norm_gains,
    layer_norm_biases,
    shift_coefficients,
    decay_offset_base,
    rate_logit_base,
    removal_key_scales,
    own_term_weights,
):
    dp, seq = lax.axis_size("dp"), lax.axis_size(SEQ)
    rank = lax.axis_index(SEQ)
    rows, width = tokens.shape[1:]
    devices = dp * seq
    own = width // devices
    ff = feedforward_key.shape[1]
    my_tokens, my_cot = tokens[0], cotangent[0]
    where = jnp.stack([rank.astype(jnp.int32), lengths[0]])

    both = lax.all_gather(jnp.stack([my_tokens, my_cot]), SEQ)
    heads_w = attention_weights.reshape(3, own, seq, LANES)
    heads_w = exchange(jnp.moveaxis(heads_w, 2, 0), SEQ)
    downs = jnp.concatenate([decay_down_matrix, rate_down_matrix, gate_down_matrix], 1)
    ups = jnp.concatenate([decay_up_matrix, rate_up_matrix, gate_up_matrix], 0).T
    vectors = jnp.concatenate(
        [
            layer_norm_gains,
            layer_norm_biases,
            shift_coefficients,
            decay_offset_base[None],
            rate_logit_base[None],
            removal_key_scales,
            own_term_weights[None],
        ],
        0,
    )
    count = vectors.shape[0]
    low = downs.shape[1]
    lane_rows = 2 * own
    vec_rows = as_rows(vectors.reshape(-1), LANES * 8).reshape(-1, LANES)
    flat = jnp.concatenate(
        [
            heads_w.reshape(-1, LANES),
            downs[:, :LANES],
            downs[:, LANES:],
            vec_rows,
            ups[:, :LANES],
            ups[:, LANES:],
        ],
        0,
    )
    flat = lax.all_gather(flat, "dp")
    cut = seq * 3 * own
    w = flat[:, :cut].reshape(devices, 3, own, LANES)
    split = cut + lane_rows + vec_rows.shape[0]
    first = lax.all_gather(flat[:, cut:split], SEQ)
    second = lax.all_gather(flat[:, split:], SEQ)

    def wide(pairs):
        pairs = pairs.reshape(seq, dp, 2, own, LANES)
        return jnp.transpose(pairs, (1, 0, 3, 2, 4)).reshape(width, low)

    down = wide(first[:, :, :lane_rows])
    start = rank * LANES
    up = lax.dynamic_slice_in_dim(wide(second), start, LANES, 0)
    vec = first[:, :, lane_rows:].reshape(seq, dp, -1)[:, :, : count * own]
    vec = jnp.transpose(vec.reshape(seq, dp, count, own), (2, 1, 0, 3))
    vec = vec.reshape(count, width).astype(F32)
    own_vec = lax.dynamic_slice_in_dim(vec, start, LANES, 1)
    own_vec = jnp.concatenate(
        [own_vec[13:18], own_vec[2:3], own_vec[5:6], jnp.zeros((1, LANES), F32)], 0
    )
    part_rows = feedforward_value.shape[0]
    key = feedforward_key.reshape(own, dp, seq, part_rows)
    key = exchange(jnp.moveaxis(key, 2, 0).reshape(seq, own, dp * part_rows), SEQ)
    key = key.reshape(2, part_rows, dp * part_rows)
    kv = lax.all_gather(
        jnp.concatenate([key[0], key[1], feedforward_value], 1), "dp", tiled=True
    )
    wo = lax.all_gather(lax.all_gather(output_weight, "dp"), SEQ)
    wo = jnp.moveaxis(wo, 1, 0).reshape(width, width)
    x = both[:, 0].reshape(seq * rows, width)
    cot = both[:, 1].reshape(seq * rows, width)
    where = jnp.stack(
        [rank.astype(jnp.int32), lengths[0], lax.axis_index("core").astype(jnp.int32)]
    )

    r, k, v, lw, rate, gv, h = project_call(x, w, down, up, vec, own_vec)
    attn, wkv, w0, uv, inverse, states = recur_call(r, k, v, lw, rate, gv, own_vec)
    mine, other = spread(attn)
    part, back, resid, gkv = ffn_call(where, x, mine, other, cot, wo, kv, vec)
    gkv = lax.psum_scatter(gkv, "dp", scatter_dimension=0, tiled=True)
    back = collect(back)
    mine_rows, other_rows = [
        lax.dynamic_slice_in_dim(item, rank * rows, rows, 1) for item in (mine, other)
    ]
    g_resid, g_in, gwo, sums1 = resid_call(
        where, back, resid, my_cot, mine_rows, other_rows, wo, vec
    )
    wo_sum = lax.psum_scatter(
        gwo.reshape(dp, seq, own, width), SEQ, scatter_dimension=1, tiled=False
    )
    g_in = exchange(g_in, SEQ).reshape(seq * rows, LANES)
    ffn_out = collect(part.reshape(seq, rows, width))
    g, sums2 = recur_back_call(
        r, k, v, lw, rate, gv, own_vec, wkv, w0, uv, inverse, states, g_in
    )
    g, gkv, ffn_out = lax.optimization_barrier((g, gkv, ffn_out))
    gkey = jnp.stack([gkv[:, : dp * part_rows], gkv[:, dp * part_rows : 2 * dp * part_rows]])
    key_sum = exchange(gkey.reshape(seq, own, dp * part_rows), SEQ)
    back2, gw, gdown, gup, coef_sums = project_back_call(x, g, h, w, down, up, vec)
    back2, wo_sum, key_sum = lax.optimization_barrier((back2, wo_sum, key_sum))
    gw = lax.psum_scatter(gw, "dp", scatter_dimension=0, tiled=True)
    wo_sum = lax.psum_scatter(wo_sum, "dp", scatter_dimension=0, tiled=False).astype(F32)
    input_grad = input_call(collect(back2), my_tokens, g_resid, vec)
    ffn_out = jnp.sum(ffn_out.astype(F32), 0)
    position = rank * rows + jnp.arange(rows, dtype=jnp.int32)
    valid = (position < lengths[0]).astype(F32)[:, None]
    output = (valid * (resid[:rows] + ffn_out)).astype(BF)
    value_sum = gkv[:, 2 * dp * part_rows :].astype(F32)
    key_sum = key_sum.reshape(seq, own, dp, part_rows)
    key_sum = jnp.transpose(key_sum, (1, 2, 0, 3)).reshape(own, ff).astype(F32)
    mix_sum = exchange(gw, SEQ)
    mix_sum = jnp.transpose(mix_sum, (1, 2, 0, 3)).reshape(3, own, width).astype(F32)

    place = partial(lax.dynamic_update_slice_in_dim, start_index=start)
    heads_vec = place(jnp.zeros((8, width), F32), sums2, axis=1)
    vec_grad = jnp.concatenate(
        [
            coef_sums[6:7],
            sums1[0:1],
            heads_vec[5:6],
            coef_sums[7:8],
            sums1[1:2],
            heads_vec[6:7],
            coef_sums[:6],
            sums1[2:3],
            heads_vec[0:5],
        ],
        0,
    ).astype(BF)
    up_grad = place(jnp.zeros((width, low), BF), gup, axis=0)

    def owners(x):
        return jnp.moveaxis(x.reshape((dp, seq, own) + x.shape[1:]), 1, 0)

    vec_grad = owners(vec_grad.T).reshape(seq, dp, -1)
    vec_grad = as_rows(vec_grad, LANES * 8).reshape(seq, dp, -1, LANES)
    pack = jnp.concatenate(
        [
            owners(gdown[:, :LANES]),
            owners(gdown[:, LANES:]),
            owners(up_grad[:, :LANES]),
            owners(up_grad[:, LANES:]),
            vec_grad,
        ],
        2,
    )
    pack = jnp.sum(exchange(pack, SEQ).astype(F32), 0).astype(BF)
    pack = jnp.sum(exchange(pack, "dp").astype(F32), 0)
    pairs = pack[: 4 * own].reshape(2, 2, own, LANES)
    pairs = jnp.moveaxis(pairs, 1, 2).reshape(2, own, low)
    down_sum, up_sum = pairs[0], pairs[1].T
    vec_sum = pack[4 * own :].reshape(-1)[: own * count].reshape(own, count).T
    cut0 = decay_down_matrix.shape[1]
    cut1 = cut0 + rate_down_matrix.shape[1]
    return (
        output[None],
        input_grad[None],
        mix_sum,
        wo_sum,
        down_sum[:, :cut0],
        up_sum[:cut0],
        down_sum[:, cut0:cut1],
        up_sum[cut0:cut1],
        down_sum[:, cut1:],
        up_sum[cut1:],
        key_sum,
        value_sum,
        vec_sum[:3],
        vec_sum[3:6],
        jnp.concatenate([vec_sum[6:7], vec_sum[8:13]], 0),
        vec_sum[7],
        vec_sum[13],
        vec_sum[14],
        vec_sum[15:17],
        vec_sum[17],
    )


def specs_of(axes):
    both = axes
    seq = axes[1:] if len(axes) > 2 else axes[1]
    row = P("dp", seq, None)
    first = P(both, None)
    second = P(None, both)
    vector = P(both)
    ins = (row, P("dp"), row, P(None, both, None)) + (first,)
    ins += (first, second, first, second, first, second, first, first)
    ins += (second, second, second, vector, vector, second, vector)
    outs = (row, row, P(None, both, None), first)
    outs += (first, second, first, second, first, second, first, first)
    outs += (second, second, second, vector, vector, vector, second, vector)
    return ins, outs


def solution(mesh):
    dp, seq = mesh.shape["dp"], mesh.shape["seq"]
    by_heads = HEADS * HEAD_SIZE // seq == LANES
    if by_heads:
        mesh = Mesh(mesh.devices.reshape(dp, seq // 2, 2), ALL)
    ins, outs = specs_of(ALL if by_heads else BOTH)
    run = local_slot if by_heads else local
    return jax.shard_map(run, mesh=mesh, in_specs=ins, out_specs=outs, check_vma=False)
```

```python
from functools import partial

import jax
import jax.numpy as jnp
from jax import lax
from jax.experimental import pallas as pl
from jax.experimental.pallas import tpu as pltpu
from jax.sharding import Mesh
from jax.sharding import PartitionSpec as P

HEAD_SIZE = 64
HEADS = 16
BOTH = ("dp", "seq")

HIGH = lax.Precision.HIGHEST
LN_EPS = 1e-05
GN_EPS = 0.00064
NORM_EPS = 1e-06
F32 = jnp.float32
BF = jnp.bfloat16
PASSES = 3


def shifted(value, axis, steps):
    count = lax.axis_size(axis)
    first, last = (max(0, -steps), min(count, count - steps))
    return lax.ppermute(value, axis, [(source, source + steps) for source in range(first, last)])


def layer_norm(content_entries, gain, bias):
    center = content_entries - jnp.mean(content_entries, -1, keepdims=True)
    spread = jnp.mean(center * center, -1, keepdims=True)
    return center * lax.rsqrt(spread + LN_EPS) * gain + bias


def token_mix(standardized_entries, left_edge, coefs):
    previous = jnp.concatenate([left_edge, standardized_entries[:, :-1]], 1)
    delta = previous - standardized_entries
    return tuple(
        (standardized_entries + delta * coefs[coef_index] for coef_index in range(coefs.shape[0]))
    )


def prepare_inputs(keys_raw, decay_lora, rate_lora, decay_base, rate_base, key_scales):
    log_decay = -jnp.exp(-jax.nn.softplus(-(decay_base + decay_lora)) - 0.5)
    rate = jax.nn.sigmoid(rate_base + rate_lora)
    scaled = (keys_raw * key_scales[0]).reshape(keys_raw.shape[:-1] + (HEADS, HEAD_SIZE))
    unit = scaled * lax.rsqrt(jnp.sum(scaled * scaled, -1, keepdims=True) + NORM_EPS)
    unit = unit.reshape(keys_raw.shape)
    keys_fin = keys_raw * (1.0 + (rate - 1.0) * key_scales[1])
    return log_decay, keys_fin, unit, unit * rate


def combined_result(wkv, receptance, keys_fin, values, gate_value, own_weights, gain, bias):
    split = wkv.shape[:-1] + (HEADS, HEAD_SIZE)
    heads = wkv.reshape(split)
    center = heads - jnp.mean(heads, -1, keepdims=True)
    spread = jnp.mean(center * center, -1, keepdims=True)
    normed = (center * lax.rsqrt(spread + GN_EPS)).reshape(wkv.shape) * gain + bias
    own = jnp.sum((receptance * keys_fin * own_weights).reshape(split), -1, keepdims=True)
    return (normed + (own * values.reshape(split)).reshape(wkv.shape)) * gate_value


def dg(a,b,ca,cb):
    return lax.dot_general(a,b,(((ca,),(cb,)),((),())),preferred_element_type=F32)

def mm(a,b,ca=1,cb=0,passes=1):
    if passes==1:
        return dg(a.astype(BF),b.astype(BF),ca,cb)
    ah=a.astype(BF); bh=b.astype(BF)
    al=(a-ah.astype(F32)).astype(BF); bl=(b-bh.astype(F32)).astype(BF)
    return dg(jnp.concatenate([ah,ah,al],ca),jnp.concatenate([bh,bl,bh],cb),ca,cb)

def iota(shape,d): return lax.broadcasted_iota(jnp.int32,shape,d)

def lanes(n):
    lane=iota((1,n),1)
    return (lane<n//2).astype(F32),(lane>=n//2).astype(F32)

def halves(x,m0,m1):
    return jnp.concatenate([x*m0,x*m1],0)

def compact(g,m0,m1):
    h=g.shape[0]//2
    return g[:h]*m0+g[h:]*m1

def scaled_inputs(r,k,kk,b,lw):
    n=lw.shape[0]
    tri=(iota((n,n),0)>=iota((n,n),1)).astype(F32)
    cum=lax.dot_general(tri,lw,(((1,),(0,)),((),())),precision=HIGH,preferred_element_type=F32)
    total=cum[n-1:n]
    center=0.5*total
    up=jnp.exp(cum-center)
    upx=jnp.exp(cum-lw-center)
    down=jnp.exp(center-cum)
    at=-kk*upx; rt=r*up; bt=b*down; kt=k*down
    return at,rt,bt,kt,center,total,up,upx,down

def score_mask(n):
    t=iota((2*n,2*n),0); s=iota((2*n,2*n),1)
    low=t<n
    tt=jnp.where(low,t,t-n); ss=jnp.where(s<n,s,s-n)
    return (ss<tt)|((ss==tt)&jnp.logical_not(low))

def invert(a,passes):
    n=a.shape[0]
    t=iota((n,n),0); s=iota((n,n),1)
    x=t^s
    inv=jnp.where(t==s,1.0,0.0)+jnp.where((x==1),a,0.0)
    b=2
    while b<n:
        off=jnp.where((x>=b)&(x<2*b),a,0.0)
        inv=inv+mm(inv,mm(off,inv,passes=passes),passes=passes)
        b*=2
    return inv

def fwd_pair(r,k,v,kk,b,lw,pt,p):
    n=r.shape[0]; m0,m1=lanes(r.shape[1])
    at,rt,bt,kt,center,total,*_=scaled_inputs(r,k,kk,b,lw)
    x=jnp.concatenate([at,rt],0); y=jnp.concatenate([bt,kt],0)
    mask=score_mask(n)
    s0=jnp.where(mask,mm(x*m0,y,1,1,p),0.0)
    s1=jnp.where(mask,mm(x*m1,y,1,1,p),0.0)
    t0=invert(s0[:n,:n],pt); t1=invert(s1[:n,:n],pt)
    vs=halves(v,m0,m1)
    akv=mm(jnp.concatenate([s0[:n,n:],s1[:n,n:]],1),vs,passes=p)
    t01=jnp.concatenate([t0,t1],1)
    w=mm(t01,halves(at,m0,m1),passes=p); uv=mm(t01,halves(akv,m0,m1),passes=p)
    rb=jnp.concatenate([s0[n:,:n],s1[n:,:n]],1); rk=jnp.concatenate([s0[n:,n:],s1[n:,n:]],1)
    q=rt+mm(rb,halves(w,m0,m1),passes=p)
    oloc=mm(rb,halves(uv,m0,m1),passes=p)+mm(rk,vs,passes=p)
    ec=jnp.exp(center); er=jnp.exp(total-center)
    q0=q*ec; w0=w*ec
    bh=bt*er; kh=kt*er
    dfull=mm(w0,bh,0,0,p); efull=mm(uv,bh,0,0,p)+mm(v,kh,0,0,p)
    half=r.shape[1]//2
    lane=iota((half,2*half),1); row=iota((half,2*half),0)
    eye=jnp.where((lane==row)|(lane==row+half),1.0,0.0)
    d=compact(dfull,m0,m1)+eye*jnp.exp(total)
    e=compact(efull,m0,m1)
    return q0,oloc,w0,uv,t01,d,e

def bwd_pair(r,k,v,kk,b,lw,t01,w0,uv,do,s_in,ds_out,p):
    n=r.shape[0]; m0,m1=lanes(r.shape[1])
    at,rt,bt,kt,center,total,up,upx,down=scaled_inputs(r,k,kk,b,lw)
    x=jnp.concatenate([at,rt],0); y=jnp.concatenate([bt,kt],0)
    mask=score_mask(n)
    s0=jnp.where(mask,mm(x*m0,y,1,1,p),0.0)
    s1=jnp.where(mask,mm(x*m1,y,1,1,p),0.0)
    ec=jnp.exp(center); er=jnp.exp(total-center)
    stil=halves(s_in*ec,m0,m1); sraw=halves(s_in,m0,m1); dst=halves(ds_out*er,m0,m1)
    u=mm(w0,sraw,1,1,p)+uv
    dos=halves(do,m0,m1)
    du=mm(jnp.concatenate([s0[n:,:n],s1[n:,:n]],0),dos,0,0,p)+mm(bt,dst,1,1,p)
    z=mm(jnp.concatenate([t01[:,:n],t01[:,n:]],0),halves(du,m0,m1),0,0,p)
    zo=jnp.concatenate([z,do],0)
    dv=mm(s0[:,n:],zo*m0,0,0,p)+mm(s1[:,n:],zo*m1,0,0,p)+mm(kt,dst,1,1,p)
    uvs=jnp.concatenate([u,v],0)
    g0=jnp.where(mask,mm(zo*m0,uvs,1,1,p),0.0)
    g1=jnp.where(mask,mm(zo*m1,uvs,1,1,p),0.0)
    dx=mm(g0,y*m0,passes=p)+mm(g1,y*m1,passes=p)+mm(zo,stil,passes=p)
    dy=mm(g0,x*m0,0,0,p)+mm(g1,x*m1,0,0,p)+mm(uvs,dst,passes=p)
    da=dx[:n]; dr=dx[n:]; db=dy[:n]; dk=dy[n:]
    if p==1:
        rnd=lambda q: q.astype(BF).astype(F32)
    else:
        rnd=lambda q:q
    gl=rnd(rt)*dr-rnd(bt)*db-rnd(kt)*dk
    ga=rnd(at)*da
    gend=jnp.sum(rnd(dst)*(stil+mm(u,bt,0,0,p)+mm(v,kt,0,0,p)),0,keepdims=True)
    tri=(iota((n,n),0)<=iota((n,n),1)).astype(F32)
    glw=lax.dot_general(tri,gl+ga,(((1,),(0,)),((),())),precision=HIGH,preferred_element_type=F32)-ga+gend
    ds=compact(mm(zo,x,0,0,p)+dst,m0,m1)*ec
    return dr*up,dk*down,dv,-da*upx,db*down,glw,ds

def fwd_kernel(pt,p,r,k,v,kk,b,lw,q0,oloc,w0,uv,t01,d,e):
    outs=fwd_pair(r[...],k[...],v[...],kk[...],b[...],lw[...],pt,p)
    for ref,val in zip((q0,oloc,w0,uv,t01,d,e),outs): ref[...]=val.astype(ref.dtype)

def bwd_kernel(p,*refs):
    outs=bwd_pair(*[q[...].astype(F32) for q in refs[:12]],p)[:6]
    for ref,val in zip(refs[12:],outs): ref[...]=val.astype(ref.dtype)


STATE = HEAD_SIZE
PAIR = 2 * HEAD_SIZE


def specs(rows):
    col = pl.BlockSpec((rows, PAIR), lambda i: (0, i))
    state = pl.BlockSpec((STATE, PAIR), lambda i: (0, i))
    wide = pl.BlockSpec((rows, 2 * rows), lambda i: (0, i))
    return col, state, wide


def rec_forward(*args):
    n, f = args[0].shape
    pairs = f // PAIR
    col, state, wide = specs(n)
    shape = jax.ShapeDtypeStruct
    return pl.pallas_call(
        partial(fwd_kernel, PASSES, PASSES),
        grid=(pairs,),
        in_specs=[col] * 6,
        out_specs=[col] * 4 + [wide, state, state],
        out_shape=[shape((n, f), F32)] * 4
        + [shape((n, pairs * 2 * n), F32)]
        + [shape((STATE, f), F32)] * 2,
        compiler_params=pltpu.CompilerParams(vmem_limit_bytes=48 << 20),
        name="rec_forward",
    )(*args)


def rec_backward(*args):
    n, f = args[0].shape
    pairs = f // PAIR
    col, state, wide = specs(n)
    return pl.pallas_call(
        partial(bwd_kernel, PASSES),
        grid=(pairs,),
        in_specs=[col] * 6 + [wide, col, col, col, state, state],
        out_specs=[col] * 6,
        out_shape=[jax.ShapeDtypeStruct((n, f), F32)] * 6,
        compiler_params=pltpu.CompilerParams(vmem_limit_bytes=48 << 20),
        name="rec_backward",
    )(*args)


def combine_kernel(side, dl_ref, el_ref, d_ref, e_ref, dn_ref, en_ref):
    m0, m1 = lanes(PAIR)
    for pair in range(d_ref.shape[1] // PAIR):
        cols = pl.ds(pair * PAIR, PAIR)
        dl = dl_ref[:, cols].astype(F32)
        el = el_ref[:, cols].astype(F32)
        d = d_ref[:, cols]
        block = halves(d, m0, m1)
        if side == 1:
            both = mm(jnp.concatenate([dl, el], 0), block, passes=PASSES)
            dn_ref[:, cols] = both[:STATE]
            en_ref[:, cols] = both[STATE:] + e_ref[:, cols]
        else:
            en_ref[:, cols] = mm(el, block, 1, 1, passes=PASSES) + e_ref[:, cols]
            right = halves(dl, m0, m1)
            dn_ref[:, cols] = mm(d, right, passes=PASSES)


def combine(side, dl, el, d, e):
    return pl.pallas_call(
        partial(combine_kernel, side),
        out_shape=[jax.ShapeDtypeStruct(d.shape, F32)] * 2,
        compiler_params=pltpu.CompilerParams(vmem_limit_bytes=32 << 20),
        name="combine_states",
    )(dl, el, d, e)


def scan_states(transfer, offset, side):
    count = lax.axis_size("seq")

    def move(value, steps):
        return shifted(value.astype(BF), "seq", side * steps)

    d, e = move(transfer, 1).astype(F32), move(offset, 1).astype(F32)
    reach = 1
    while reach < count - 1:
        d, e = combine(side, move(d, reach), move(e, reach), d, e)
        reach *= 2
    return e


def apply_state_kernel(q_ref, s_ref, o_ref, out_ref):
    m0, m1 = lanes(PAIR)
    for pair in range(q_ref.shape[1] // PAIR):
        cols = pl.ds(pair * PAIR, PAIR)
        block = halves(s_ref[:, cols], m0, m1)
        out_ref[:, cols] = o_ref[:, cols] + mm(q_ref[:, cols], block, 1, 1, passes=PASSES)


def apply_state(q, s, o):
    return pl.pallas_call(
        apply_state_kernel,
        out_shape=jax.ShapeDtypeStruct(q.shape, F32),
        compiler_params=pltpu.CompilerParams(vmem_limit_bytes=32 << 20),
        name="apply_state",
    )(q, s, o)


def back_offset_kernel(do_ref, q_ref, f_ref):
    m0, m1 = lanes(PAIR)
    for pair in range(q_ref.shape[1] // PAIR):
        cols = pl.ds(pair * PAIR, PAIR)
        f_ref[:, cols] = compact(mm(do_ref[:, cols], q_ref[:, cols], 0, 0, PASSES), m0, m1)


def back_offset(do, q):
    return pl.pallas_call(
        back_offset_kernel,
        out_shape=jax.ShapeDtypeStruct((STATE, q.shape[1]), F32),
        compiler_params=pltpu.CompilerParams(vmem_limit_bytes=32 << 20),
        name="back_offset",
    )(do, q)

def input_backward(gradient, weight):
    return lax.dot_general(
        gradient, weight, (((1,), (1,)), ((), ())), preferred_element_type=jnp.float32
    )


def weight_backward(inputs, gradient):
    return lax.dot_general(
        inputs, gradient, (((0,), (0,)), ((), ())), preferred_element_type=jnp.float32
    )


def project(inputs, weight):
    return jnp.dot(inputs, weight, preferred_element_type=jnp.float32)


def gather_rows(packed):
    return lax.all_gather(packed, BOTH, axis=0, tiled=False)


def scatter_rows(packed):
    dp, seq = lax.axis_size("dp"), lax.axis_size("seq")
    packed = packed.reshape((dp, seq) + packed.shape[1:])
    over_seq = lax.psum_scatter(packed, "seq", scatter_dimension=1, tiled=False)
    return lax.psum_scatter(over_seq, "dp", scatter_dimension=0, tiled=False)


def as_rows(flat, width):
    rows = -(-flat.shape[-1] // width)
    padding = [(0, 0)] * (flat.ndim - 1) + [(0, rows * width - flat.shape[-1])]
    return jnp.pad(flat, padding).reshape(flat.shape[:-1] + (rows, width))


def local(
    tokens,
    lengths,
    cotangent,
    attention_weights,
    output_weight,
    decay_down_matrix,
    decay_up_matrix,
    rate_down_matrix,
    rate_up_matrix,
    gate_down_matrix,
    gate_up_matrix,
    feedforward_key,
    feedforward_value,
    layer_norm_gains,
    layer_norm_biases,
    shift_coefficients,
    decay_offset_base,
    rate_logit_base,
    removal_key_scales,
    own_term_weights,
):
    slot_count, block_len, width = tokens.shape
    rows = slot_count * block_len
    own = output_weight.shape[0]
    devices = width // own
    ranks = (decay_down_matrix.shape[1], rate_down_matrix.shape[1], gate_down_matrix.shape[1])
    low = sum(ranks)
    cut0, cut1 = ranks[0], ranks[0] + ranks[1]

    downs = jnp.concatenate([decay_down_matrix, rate_down_matrix, gate_down_matrix], 1)
    ups = jnp.concatenate([decay_up_matrix, rate_up_matrix, gate_up_matrix], 0)
    vectors = jnp.concatenate(
        [
            layer_norm_gains,
            layer_norm_biases,
            shift_coefficients,
            decay_offset_base[None],
            rate_logit_base[None],
            removal_key_scales,
            own_term_weights[None],
        ],
        0,
    )
    vector_count = vectors.shape[0]
    small = as_rows(
        jnp.concatenate([downs.reshape(-1), ups.reshape(-1), vectors.reshape(-1)]), width
    )
    packed = jnp.concatenate([attention_weights.reshape(-1, width), output_weight, small], 0)
    gathered = gather_rows(packed)
    weight_r, weight_k, weight_v, weight_o = [
        gathered[:, j * own : (j + 1) * own].reshape(width, width) for j in range(4)
    ]
    rest = gathered[:, 4 * own :].reshape(devices, -1)
    down = rest[:, : own * low].reshape(width, low)
    up = jnp.moveaxis(rest[:, own * low : 2 * own * low].reshape(devices, low, own), 0, 1)
    up = up.reshape(low, width)
    vecs = rest[:, 2 * own * low :][:, : vector_count * own].reshape(devices, vector_count, own)
    vecs = jnp.moveaxis(vecs, 0, 1).reshape(vector_count, width).astype(F32)
    gains, biases, coefs = vecs[:3], vecs[3:6], vecs[6:13]
    decay_base, rate_base, key_scales, own_weights = vecs[13], vecs[14], vecs[15:17], vecs[17]
    ffn_key = lax.all_gather(feedforward_key, BOTH, axis=0, tiled=True)
    ffn_value = lax.all_gather(feedforward_value, BOTH, axis=0, tiled=True)

    first_pos = lax.axis_index("seq") * block_len
    positions = first_pos + jnp.arange(block_len, dtype=jnp.int32)
    valid_mask = (positions[None, :] < lengths[:, None]).astype(jnp.float32)[:, :, None]
    inputs = tokens.astype(jnp.float32)
    normed, norm_pull = jax.vjp(layer_norm, inputs, gains[0], biases[0])
    left_edge = shifted(normed[:, -1:], "seq", 1)
    mixed_rows, mix_pull = jax.vjp(token_mix, normed, left_edge, coefs[:6])
    recep_mix, decay_mix, key_mix, value_mix, rate_mix, gate_mix = [
        item.reshape(rows, width).astype(BF) for item in mixed_rows
    ]
    receptance = project(recep_mix, weight_r)
    keys_raw = project(key_mix, weight_k)
    values = project(value_mix, weight_v)
    decay_tanh = jnp.tanh(project(decay_mix, down[:, :cut0]))
    decay_hidden = decay_tanh.astype(BF)
    decay_lora = project(decay_hidden, up[:cut0])
    rate_hidden = project(rate_mix, down[:, cut0:cut1]).astype(BF)
    rate_lora = project(rate_hidden, up[cut0:cut1])
    gate_sig = jax.nn.sigmoid(project(gate_mix, down[:, cut1:]))
    gate_low = gate_sig.astype(BF)
    gate_value = project(gate_low, up[cut1:])
    prepared, prep_pull = jax.vjp(
        prepare_inputs, keys_raw, decay_lora, rate_lora, decay_base, rate_base, key_scales
    )
    log_decay, keys_fin, unit, unit_rate = prepared
    streams = (receptance, keys_fin, values, unit, unit_rate, log_decay)
    q0, o_local, w0, uv, inverse, transfer, offset = rec_forward(*streams)
    state_in = scan_states(transfer, offset, 1)
    wkv = apply_state(q0, state_in, o_local)
    attn_pre, combine_pull = jax.vjp(
        combined_result,
        wkv,
        receptance,
        keys_fin,
        values,
        gate_value,
        own_weights,
        gains[2],
        biases[2],
    )
    attn_in = attn_pre.astype(BF)
    resid = inputs + project(attn_in, weight_o).reshape(inputs.shape)
    normed_ffn, norm_ffn_pull = jax.vjp(layer_norm, resid, gains[1], biases[1])
    ffn_edge = shifted(normed_ffn[:, -1:], "seq", 1)
    ffn_rows, ffn_pull = jax.vjp(token_mix, normed_ffn, ffn_edge, coefs[6:])
    ffn_mix = ffn_rows[0].reshape(rows, width).astype(BF)
    ffn_hidden = project(ffn_mix, ffn_key)
    ffn_act = jnp.square(jax.nn.relu(ffn_hidden)).astype(BF)
    ffn_result = project(ffn_act, ffn_value).reshape(inputs.shape)
    output = (valid_mask * (resid + ffn_result)).astype(BF)

    grad_out = valid_mask * cotangent.astype(jnp.float32)
    grad_ffn = grad_out.reshape(rows, width).astype(BF)
    grad_ffn_value = weight_backward(ffn_act, grad_ffn)
    grad_hidden = (
        input_backward(grad_ffn, ffn_value) * 2.0 * jax.nn.relu(ffn_hidden)
    ).astype(BF)
    grad_ffn_key = weight_backward(ffn_mix, grad_hidden)
    key_sum = scatter_rows(grad_ffn_key.astype(BF).reshape(devices, own, -1))
    value_sum = scatter_rows(
        grad_ffn_value.astype(BF).reshape(devices, feedforward_value.shape[0], width)
    )
    grad_ffn_mix = input_backward(grad_hidden, ffn_key).reshape(inputs.shape)
    grad_normed_ffn, grad_ffn_edge, grad_coef_ffn = ffn_pull((grad_ffn_mix,))
    returned_ffn = shifted(grad_ffn_edge, "seq", -1)
    grad_normed_ffn = grad_normed_ffn.at[:, -1:].add(returned_ffn)
    grad_resid, grad_gain_ffn, grad_bias_ffn = norm_ffn_pull(grad_normed_ffn)
    grad_resid = grad_resid + grad_out
    grad_attn = grad_resid.reshape(rows, width).astype(BF)
    grad_out_weight = weight_backward(attn_in, grad_attn)
    grad_attn_pre = input_backward(grad_attn, weight_o)
    (
        grad_wkv,
        direct_recep,
        direct_keys,
        direct_values,
        grad_gate_value,
        grad_own,
        grad_group_gain,
        grad_group_bias,
    ) = combine_pull(grad_attn_pre)
    grad_state = scan_states(transfer, back_offset(grad_wkv, q0), -1)
    back_recep, back_keys, back_values, back_unit, back_rate, back_decay = rec_backward(
        *streams, inverse, w0, uv, grad_wkv, state_in, grad_state
    )
    grad_keys_raw, grad_dl, grad_rl, grad_decay_base, grad_rate_base, grad_key_scales = prep_pull(
        (back_decay, back_keys + direct_keys, back_unit, back_rate)
    )
    low_recep = (back_recep + direct_recep).astype(BF)
    low_keys = grad_keys_raw.astype(BF)
    low_values = (back_values + direct_values).astype(BF)
    grad_mix = [
        weight_backward(recep_mix, low_recep),
        weight_backward(key_mix, low_keys),
        weight_backward(value_mix, low_values),
    ]
    grad_recep_mix = input_backward(low_recep, weight_r)
    grad_key_mix = input_backward(low_keys, weight_k)
    grad_value_mix = input_backward(low_values, weight_v)
    low_dl = grad_dl.astype(BF)
    grad_decay_up = weight_backward(decay_hidden, low_dl)
    low_dh = (input_backward(low_dl, up[:cut0]) * (1.0 - decay_tanh * decay_tanh)).astype(BF)
    grad_decay_down = weight_backward(decay_mix, low_dh)
    grad_decay_mix = input_backward(low_dh, down[:, :cut0])
    low_rl = grad_rl.astype(BF)
    grad_rate_up = weight_backward(rate_hidden, low_rl)
    low_rh = input_backward(low_rl, up[cut0:cut1]).astype(BF)
    grad_rate_down = weight_backward(rate_mix, low_rh)
    grad_rate_mix = input_backward(low_rh, down[:, cut0:cut1])
    low_gv = grad_gate_value.astype(BF)
    grad_gate_up = weight_backward(gate_low, low_gv)
    low_gh = (input_backward(low_gv, up[cut1:]) * gate_sig * (1.0 - gate_sig)).astype(BF)
    grad_gate_down = weight_backward(gate_mix, low_gh)
    grad_gate_mix = input_backward(low_gh, down[:, cut1:])
    grad_mixed = tuple(
        item.reshape(inputs.shape)
        for item in (
            grad_recep_mix,
            grad_decay_mix,
            grad_key_mix,
            grad_value_mix,
            grad_rate_mix,
            grad_gate_mix,
        )
    )
    grad_normed, grad_left_edge, grad_coef_mix = mix_pull(grad_mixed)
    returned_mix = shifted(grad_left_edge, "seq", -1)
    grad_normed = grad_normed.at[:, -1:].add(returned_mix)
    grad_inputs, grad_gain_mix, grad_bias_mix = norm_pull(grad_normed)
    input_grad = (grad_resid + grad_inputs).astype(BF)

    def by_device(array):
        return array.astype(BF).reshape(devices, own, -1)

    grad_downs = jnp.concatenate([grad_decay_down, grad_rate_down, grad_gate_down], 1)
    grad_ups = jnp.concatenate([grad_decay_up, grad_rate_up, grad_gate_up], 0)
    grad_vecs = jnp.stack(
        [
            grad_gain_mix,
            grad_gain_ffn,
            grad_group_gain,
            grad_bias_mix,
            grad_bias_ffn,
            grad_group_bias,
            *grad_coef_mix,
            *grad_coef_ffn,
            grad_decay_base,
            grad_rate_base,
            *grad_key_scales,
            grad_own,
        ]
    )

    def by_column(array):
        return jnp.moveaxis(array.astype(BF).reshape(-1, devices, own), 1, 0).reshape(devices, -1)

    grad_small = as_rows(
        jnp.concatenate(
            [
                grad_downs.astype(BF).reshape(devices, -1),
                by_column(grad_ups),
                by_column(grad_vecs),
            ],
            1,
        ),
        width,
    )
    sums = scatter_rows(
        jnp.concatenate([by_device(item) for item in (*grad_mix, grad_out_weight)] + [grad_small], 1)
    ).astype(F32)
    mix_sum = sums[: 3 * own].reshape(3, own, width)
    out_sum = sums[3 * own : 4 * own]
    flat = sums[4 * own :].reshape(-1)
    down_sum = flat[: own * low].reshape(own, low)
    up_sum = flat[own * low : 2 * own * low].reshape(low, own)
    vec_sum = flat[2 * own * low :][: vector_count * own].reshape(vector_count, own)
    return (
        output,
        input_grad,
        mix_sum,
        out_sum,
        down_sum[:, :cut0],
        up_sum[:cut0],
        down_sum[:, cut0:cut1],
        up_sum[cut0:cut1],
        down_sum[:, cut1:],
        up_sum[cut1:],
        key_sum.astype(F32),
        value_sum.astype(F32),
        vec_sum[:3],
        vec_sum[3:6],
        jnp.concatenate([vec_sum[6:7], vec_sum[8:13]], 0),
        vec_sum[7],
        vec_sum[13],
        vec_sum[14],
        vec_sum[15:17],
        vec_sum[17],
    )


SEQ = ("chip", "core")
ALL = ("dp", "chip", "core")
LANES = 128
E_HALF = 1.6487212707001282


def params(limit=56):
    return pltpu.CompilerParams(
        dimension_semantics=("arbitrary",), vmem_limit_bytes=limit << 20
    )


def cost(us):
    return pl.CostEstimate(flops=int(us * 10**7), bytes_accessed=int(us * 10**4), transcendentals=0)


def whole(shape):
    return pl.BlockSpec(shape, lambda i: (0,) * len(shape))


def nt(a, b):
    return dg(a.astype(BF), b.astype(BF), 1, 1)


def nn(a, b):
    return dg(a.astype(BF), b.astype(BF), 1, 0)


def tn(a, b):
    return dg(a.astype(BF), b.astype(BF), 0, 0)


def head_sum(x, m0, m1):
    s0 = jnp.sum(x * m0, -1, keepdims=True)
    s1 = jnp.sum(x * m1, -1, keepdims=True)
    return s0 * m0 + s1 * m1


def norm_parts(x):
    center = x - jnp.mean(x, -1, keepdims=True)
    rstd = lax.rsqrt(jnp.mean(center * center, -1, keepdims=True) + LN_EPS)
    return center * rstd, rstd


def shift_down(x, first):
    rolled = pltpu.roll(x, 1, 0)
    return jnp.where(iota(x.shape, 0) == 0, first, rolled)


def shift_up(x):
    n = x.shape[0]
    rolled = pltpu.roll(x, n - 1, 0)
    return jnp.where(iota(x.shape, 0) == n - 1, 0.0, rolled)


def low_act(h, m0):
    return jnp.where(m0 > 0, jnp.tanh(h), h)


def rows_of(x_ref):
    return x_ref[...].reshape(-1, x_ref.shape[-1])


def gathered(which, width, devices=2):
    return pl.BlockSpec((devices, None, LANES, width), lambda i: (i, which, 0, 0))


BLOCKS = 5


def block_of(j):
    return slice(j * LANES, (j + 1) * LANES)


def mix_columns(vec_ref):
    lane = iota((8, BLOCKS * LANES), 1)
    part = lane // LANES
    wanted = jnp.where(part == 0, 0, part + 1)
    wanted = jnp.where(part == 3, jnp.where(lane % LANES < LANES // 2, 1, 4), wanted)
    pick = (iota((8, BLOCKS * LANES), 0) == wanted).astype(BF)
    return tn(vec_ref[6:14], pick)


def column(vec_ref, row):
    pick = (iota((8, LANES), 0) == row).astype(BF)
    return tn(vec_ref[0:8], pick)


def project_kernel(x_ref, flat_ref, first_ref, up_ref, vec_ref, own_ref, *rest):
    r_ref, k_ref, v_ref, lw_ref, rate_ref, gv_ref, h_ref, wc_ref, carry = rest
    width = x_ref.shape[-1]
    m0, m1 = lanes(LANES)

    @pl.when(pl.program_id(0) == 0)
    def _():
        carry[...] = jnp.zeros_like(carry)
        seq, dp = first_ref.shape[:2]
        own = width // (seq * dp)
        for d in range(dp):
            for s in range(seq):
                at = slice((d * seq + s) * own, (d * seq + s + 1) * own)
                for j in range(3):
                    row = (3 * s + j) * own
                    wc_ref[at, block_of(j)] = flat_ref[d, row : row + own]
                for j in range(2):
                    wc_ref[at, block_of(3 + j)] = first_ref[s, d, j * own : (j + 1) * own]
        mixed = mix_columns(vec_ref) * wc_ref[:width].astype(F32)
        wc_ref[width:] = mixed.astype(BF)

    unit, _ = norm_parts(rows_of(x_ref).astype(F32))
    normed = unit * vec_ref[0:1] + vec_ref[3:4]
    delta = shift_down(normed, carry[0:1]) - normed
    carry[...] = jnp.broadcast_to(normed[-1:], carry.shape)
    out = nn(normed, wc_ref[:width]) + nn(delta, wc_ref[width:])
    r_ref[...] = out[:, block_of(0)]
    k_ref[...] = out[:, block_of(1)]
    v_ref[...] = out[:, block_of(2)]
    h_low, h_gate = out[:, block_of(3)], out[:, block_of(4)]
    h_ref[:, :LANES] = h_low
    h_ref[:, LANES:] = h_gate
    act = low_act(h_low, m0).astype(BF).astype(F32)
    dl = nt(act * m0, up_ref[:, :LANES])
    rl = nt(act * m1, up_ref[:, :LANES])
    gv_ref[...] = nt(jax.nn.sigmoid(h_gate), up_ref[:, LANES:])
    lw_ref[...] = jax.nn.sigmoid(own_ref[0:1] + dl) * (-1.0 / E_HALF)
    rate_ref[...] = jax.nn.sigmoid(own_ref[1:2] + rl)


def key_parts(kraw, rate, own_ref, m0, m1):
    scaled = kraw * own_ref[2:3]
    rs = lax.rsqrt(head_sum(scaled * scaled, m0, m1) + NORM_EPS)
    unit = scaled * rs
    keys = kraw * (1.0 + (rate - 1.0) * own_ref[3:4])
    return unit, rs, keys


def group_norm(wkv, m0, m1):
    center = wkv - head_sum(wkv, m0, m1) * (1.0 / HEAD_SIZE)
    spread = head_sum(center * center, m0, m1) * (1.0 / HEAD_SIZE)
    rstd = lax.rsqrt(spread + GN_EPS)
    return center * rstd, rstd


def invert_all(mats, passes):
    n = mats[0].shape[0]
    t, s = iota((n, n), 0), iota((n, n), 1)
    x = t ^ s
    inv = [jnp.where(t == s, 1.0, 0.0) + jnp.where(x == 1, a, 0.0) for a in mats]
    b = 2
    while b < n:
        near = (x >= b) & (x < 2 * b)
        half = [mm(jnp.where(near, a, 0.0), i, passes=passes) for a, i in zip(mats, inv)]
        inv = [i + mm(i, h, passes=passes) for i, h in zip(inv, half)]
        b *= 2
    return inv


def each(f, *lists):
    return [f(*items) for items in zip(*lists)]


def fwd_chunks(r, k, v, kk, b, lw, p):
    n = r[0].shape[0]
    m0, m1 = lanes(LANES)
    parts = each(scaled_inputs, r, k, kk, b, lw)
    at, rt, bt, kt, center, total = [[q[i] for q in parts] for i in range(6)]
    x = each(lambda a, c: jnp.concatenate([a, c], 0), at, rt)
    y = each(lambda a, c: jnp.concatenate([a, c], 0), bt, kt)
    mask = score_mask(n)
    s0 = each(lambda a, c: jnp.where(mask, mm(a * m0, c, 1, 1, p), 0.0), x, y)
    s1 = each(lambda a, c: jnp.where(mask, mm(a * m1, c, 1, 1, p), 0.0), x, y)
    inv = invert_all([q[:n, :n] for q in s0] + [q[:n, :n] for q in s1], p)
    t01 = each(lambda a, c: jnp.concatenate([a, c], 1), inv[: len(r)], inv[len(r) :])

    def side(lo, hi, left, right):
        return each(
            lambda a, c: jnp.concatenate([a[lo:hi, left:right], c[lo:hi, left:right]], 1), s0, s1
        )

    vs = each(lambda a: halves(a, m0, m1), v)
    akv = each(lambda a, c: mm(a, c, passes=p), side(0, n, n, 2 * n), vs)
    w = each(lambda t, a: mm(t, halves(a, m0, m1)), t01, at)
    uv = each(lambda t, a: mm(t, halves(a, m0, m1), passes=p), t01, akv)
    rb, rk = side(n, 2 * n, 0, n), side(n, 2 * n, n, 2 * n)
    q = each(lambda a, c, d: a + mm(c, halves(d, m0, m1)), rt, rb, w)
    oloc = each(lambda c, d: mm(c, halves(d, m0, m1), passes=p), rb, uv)
    oloc = each(lambda a, c, d: a + mm(c, d, passes=p), oloc, rk, vs)
    ec = each(jnp.exp, center)
    er = each(lambda a, c: jnp.exp(a - c), total, center)
    q0 = each(jnp.multiply, q, ec)
    w0 = each(jnp.multiply, w, ec)
    bh = each(jnp.multiply, bt, er)
    kh = each(jnp.multiply, kt, er)
    dfull = each(lambda a, c: mm(a, c, 0, 0), w0, bh)
    efull = each(lambda a, c, d, f: mm(a, c, 0, 0, p) + mm(d, f, 0, 0, p), uv, bh, v, kh)
    half = STATE
    lane, row = iota((half, 2 * half), 1), iota((half, 2 * half), 0)
    eye = jnp.where((lane == row) | (lane == row + half), 1.0, 0.0)
    d = each(lambda a, c: compact(a, m0, m1) + eye * jnp.exp(c), dfull, total)
    e = each(lambda a: compact(a, m0, m1), efull)
    return q0, oloc, w0, uv, t01, d, e


def bwd_chunks(r, k, v, kk, b, lw, t01, w0, uv, do, s_in, ds_out, p):
    n = r[0].shape[0]
    m0, m1 = lanes(LANES)
    parts = each(scaled_inputs, r, k, kk, b, lw)
    at, rt, bt, kt, center, total, up, upx, down = [[q[i] for q in parts] for i in range(9)]
    stack = lambda a, c: jnp.concatenate([a, c], 0)
    x, y = each(stack, at, rt), each(stack, bt, kt)
    mask = score_mask(n)
    s0 = each(lambda a, c: jnp.where(mask, mm(a * m0, c, 1, 1, p), 0.0), x, y)
    s1 = each(lambda a, c: jnp.where(mask, mm(a * m1, c, 1, 1, p), 0.0), x, y)
    ec = each(jnp.exp, center)
    er = each(lambda a, c: jnp.exp(a - c), total, center)
    stil = each(lambda a, c: halves(a * c, m0, m1), s_in, ec)
    sraw = each(lambda a: halves(a, m0, m1), s_in)
    dst = each(lambda a, c: halves(a * c, m0, m1), ds_out, er)
    u = each(lambda a, c, d: mm(a, c, 1, 1) + d, w0, sraw, uv)
    dos = each(lambda a: halves(a, m0, m1), do)
    du = each(lambda a, c, d: mm(stack(a[n:, :n], c[n:, :n]), d, 0, 0, p), s0, s1, dos)
    du = each(lambda a, c, d: a + mm(c, d, 1, 1), du, bt, dst)
    z = each(lambda t, a: mm(stack(t[:, :n], t[:, n:]), halves(a, m0, m1), 0, 0, p), t01, du)
    zo = each(stack, z, do)
    dv = each(lambda a, c: mm(a[:, n:], c * m0, 0, 0, p), s0, zo)
    dv = each(lambda a, c, d: a + mm(c[:, n:], d * m1, 0, 0, p), dv, s1, zo)
    dv = each(lambda a, c, d: a + mm(c, d, 1, 1), dv, kt, dst)
    uvs = each(stack, u, v)
    g0 = each(lambda a, c: jnp.where(mask, mm(a * m0, c, 1, 1, p), 0.0), zo, uvs)
    g1 = each(lambda a, c: jnp.where(mask, mm(a * m1, c, 1, 1, p), 0.0), zo, uvs)
    dx = each(lambda a, c: mm(a, c * m0, passes=p), g0, y)
    dx = each(lambda o, a, c: o + mm(a, c * m1, passes=p), dx, g1, y)
    dx = each(lambda o, a, c: o + mm(a, c), dx, zo, stil)
    dy = each(lambda a, c: mm(a, c * m0, 0, 0, p), g0, x)
    dy = each(lambda o, a, c: o + mm(a, c * m1, 0, 0, p), dy, g1, x)
    dy = each(lambda o, a, c: o + mm(a, c), dy, uvs, dst)
    tri = (iota((n, n), 0) <= iota((n, n), 1)).astype(F32)
    outs = []
    for i in range(len(r)):
        da, dr, db, dk = dx[i][:n], dx[i][n:], dy[i][:n], dy[i][n:]
        gl = rt[i] * dr - bt[i] * db - kt[i] * dk
        ga = at[i] * da
        grown = stil[i] + mm(u[i], bt[i], 0, 0) + mm(v[i], kt[i], 0, 0)
        gend = jnp.sum(dst[i] * grown, 0, keepdims=True)
        glw = lax.dot_general(
            tri, gl + ga, (((1,), (0,)), ((), ())), precision=HIGH, preferred_element_type=F32
        )
        glw = glw - ga + gend
        outs.append((dr * up[i], dk * down[i], dv[i], -da * upx[i], db * down[i], glw))
    return outs


CHUNKS = 4


def recur_kernel(r_ref, k_ref, v_ref, lw_ref, rate_ref, gv_ref, own_ref, *rest):
    attn_ref, wkv_ref, w0_ref, uv_ref, inv_ref, q0_ref, st_ref, d_ref, state = rest
    m0, m1 = lanes(LANES)

    @pl.when(pl.program_id(0) == 0)
    def _():
        state[...] = jnp.zeros_like(state)

    count = r_ref.shape[0] // LANES
    at = [slice(c * LANES, (c + 1) * LANES) for c in range(count)]
    small = [slice(c * STATE, (c + 1) * STATE) for c in range(count)]
    r, v, rate = [[ref[q] for q in at] for ref in (r_ref, v_ref, rate_ref)]
    parts = [key_parts(k_ref[q], a, own_ref, m0, m1) for q, a in zip(at, rate)]
    unit, keys = [q[0] for q in parts], [q[2] for q in parts]
    q0, oloc, w0, uv, t01, d, e = fwd_chunks(
        r, keys, v, unit, each(jnp.multiply, unit, rate), [lw_ref[q] for q in at], PASSES
    )
    s = state[...]
    states = []
    for c in range(count):
        states.append(s)
        s = mm(s, halves(d[c], m0, m1), passes=PASSES) + e[c]
    state[...] = s
    wkv = each(lambda o, q, a: o + mm(q, halves(a, m0, m1), 1, 1), oloc, q0, states)
    for c in range(count):
        normed, _ = group_norm(wkv[c], m0, m1)
        bonus = head_sum(r[c] * keys[c] * own_ref[4:5], m0, m1)
        pre = normed * own_ref[5:6] + own_ref[6:7] + bonus * v[c]
        attn = (pre * gv_ref[at[c]]).astype(BF)
        for chip in range(attn_ref.shape[0]):
            attn_ref[chip, at[c]] = attn
        wkv_ref[at[c]] = wkv[c]
        w0_ref[at[c]] = w0[c]
        uv_ref[at[c]] = uv[c]
        inv_ref[at[c]] = t01[c]
        q0_ref[at[c]] = q0[c]
        st_ref[small[c]] = states[c]
        d_ref[small[c]] = d[c]


def front_kernel(x_ref, flat_ref, first_ref, up_ref, vec_ref, own_ref, *rest):
    streams, (h_ref, wc_ref), kept = rest[:6], rest[6:8], rest[8:16]
    carry, state = rest[16:]
    project_kernel(
        x_ref, flat_ref, first_ref, up_ref, vec_ref, own_ref, *streams, h_ref, wc_ref, carry
    )
    recur_kernel(*streams, own_ref, *kept, state)


def front_call(x, flat, first, up, vec, own, chips):
    n, width = x.shape[0] * LANES, x.shape[-1]
    c = LANES * CHUNKS
    block = pl.BlockSpec((c, LANES), lambda i: (i, 0))
    double = pl.BlockSpec((c, 2 * LANES), lambda i: (i, 0))
    state = pl.BlockSpec((CHUNKS * STATE, LANES), lambda i: (i, 0))
    shape = jax.ShapeDtypeStruct
    wc = shape((2 * width, BLOCKS * LANES), BF)
    one, two = shape((n, LANES), F32), shape((n, 2 * LANES), F32)
    kept = shape((n // LANES * STATE, LANES), F32)
    return pl.pallas_call(
        front_kernel,
        grid=(n // c,),
        in_specs=[gathered(0, width, CHUNKS)]
        + [whole(a.shape) for a in (flat, first, up, vec, own)],
        out_specs=[block] * 6
        + [double, whole(wc.shape)]
        + [pl.BlockSpec((chips, c, LANES), lambda i: (0, i, 0))]
        + [block] * 3
        + [double, block, state, state],
        out_shape=[one] * 6
        + [two, wc]
        + [shape((chips, n, LANES), BF)]
        + [one] * 3
        + [two, one, kept, kept],
        scratch_shapes=[pltpu.VMEM((8, width), F32), pltpu.VMEM((STATE, LANES), F32)],
        compiler_params=params(),
        cost_estimate=cost(20),
        name="front",
    )(x, flat, first, up, vec, own)


EDGE = 16


def write_pair(keep_ref, give_ref, at, core, first, second):
    rows = first.shape[0]

    @pl.when(core == 0)
    def _():
        keep_ref[at, 0:rows] = first
        give_ref[at, 0:rows] = second

    @pl.when(core != 0)
    def _():
        keep_ref[at, 0:rows] = second
        give_ref[at, 0:rows] = first


def write_edges(keep_ref, give_ref, step, core, inner, outer):
    rows = LANES
    blank = jnp.zeros_like(outer)
    before = jnp.maximum(step - 1, 0)

    @pl.when(core == 0)
    def _():
        keep_ref[step, rows:] = inner
        give_ref[step, rows:] = blank

    @pl.when(core != 0)
    def _():
        give_ref[step, rows:] = inner
        keep_ref[step, rows:] = blank

    @pl.when((step > 0) & (core == 0))
    def _():
        give_ref[before, rows:] = outer

    @pl.when((step > 0) & (core != 0))
    def _():
        keep_ref[before, rows:] = outer


def ffn_kernel(
    where_ref, x_ref, mine_ref, other_ref, cot_ref, wo_mine_ref, wo_other_ref, kv_ref, *rest
):
    vec_ref, keep_ref, give_ref, resid_ref, wo_ref, mix_ref, act_ref, hid_ref, *rest = rest
    carry, key_ref = rest
    step = pl.program_id(0)
    width = x_ref.shape[-1]
    rows = 2 * LANES
    ff = kv_ref.shape[0]
    value_ref = kv_ref.at[:, width:]
    core = where_ref[2]
    chips = mine_ref.shape[0]
    _, dp, _, own, _ = wo_mine_ref.shape

    @pl.when(step == 0)
    def _():
        for q in range(chips):
            for d in range(dp):
                for ref, side in ((wo_mine_ref, core), (wo_other_ref, 1 - core)):
                    row = ((d * chips + q) * 2 + side) * own
                    head = row // LANES
                    place = (head // 2 * 2 + (head + core) % 2) * LANES + row % LANES
                    block = jnp.concatenate([ref[q, d, j] for j in range(width // LANES)], 1)
                    wo_ref[pl.ds(pl.multiple_of(place, own), own)] = block
        for part in range(width // LANES):
            key_ref[part * LANES : (part + 1) * LANES] = kv_ref[
                part // 2 * LANES : (part // 2 + 1) * LANES, part % 2 * ff : (part % 2 + 1) * ff
            ]
        carry[...] = jnp.zeros_like(carry)

    attn = jnp.concatenate(
        [ref[q] for q in range(chips) for ref in (mine_ref, other_ref)], 1
    )
    resid = rows_of(x_ref).astype(F32) + nn(attn, wo_ref[...])
    for half in range(2):
        block = 2 * step + half

        @pl.when(block == where_ref[0])
        def _(half=half):
            resid_ref[0:LANES] = resid[half * LANES : (half + 1) * LANES]

        @pl.when(block == where_ref[0] - 1)
        def _(half=half):
            resid_ref[LANES:] = resid[half * LANES : (half + 1) * LANES]

    unit, _ = norm_parts(resid)
    normed = unit * vec_ref[1:2] + vec_ref[4:5]
    mix = (normed + (shift_down(normed, carry[0:1]) - normed) * vec_ref[12:13]).astype(BF)
    carry[...] = jnp.broadcast_to(normed[-1:], carry.shape)
    relu = jnp.maximum(nn(mix, key_ref[...]), 0.0)
    act = (relu * relu).astype(BF)
    position = step * rows + iota((rows, 1), 0)
    g_ffn = jnp.where(position < where_ref[1], rows_of(cot_ref), jnp.zeros((), BF))
    g_hidden = (nt(g_ffn, value_ref[...]) * 2.0 * relu).astype(BF)
    g_mix = nt(g_hidden, key_ref[...]).astype(BF)
    write_pair(keep_ref, give_ref, step, core, g_mix[:LANES], g_mix[LANES:])
    write_edges(
        keep_ref, give_ref, step, core, g_mix[LANES : LANES + EDGE], g_mix[:EDGE]
    )
    mix_ref[...] = mix
    act_ref[...] = act
    hid_ref[...] = g_hidden


def ffn_weights_kernel(where_ref, cot_ref, mix_ref, act_ref, hid_ref, value_ref, *rest):
    keep_ref, give_ref, gkv_ref, acc_key, acc_value = rest
    step = pl.program_id(0)
    width = cot_ref.shape[-1]
    rows = 2 * LANES
    ff = value_ref.shape[0]

    @pl.when(step == 0)
    def _():
        acc_key[...] = jnp.zeros_like(acc_key)
        acc_value[...] = jnp.zeros_like(acc_value)

    act = act_ref[...]
    position = step * rows + iota((rows, 1), 0)
    g_ffn = jnp.where(position < where_ref[1], rows_of(cot_ref), jnp.zeros((), BF))
    part = nn(act, value_ref[...]).astype(BF)
    write_pair(keep_ref, give_ref, 0, where_ref[2], part[:LANES], part[LANES:])
    acc_value[...] += tn(act, g_ffn)
    acc_key[...] += tn(mix_ref[...], hid_ref[...])

    @pl.when(step == pl.num_programs(0) - 1)
    def _():
        gkv_ref[:, width:] = acc_value[...].astype(BF)
        for part in range(width // LANES):
            gkv_ref[
                part // 2 * LANES : (part // 2 + 1) * LANES, part % 2 * ff : (part % 2 + 1) * ff
            ] = acc_key[part * LANES : (part + 1) * LANES].astype(BF)


def ffn_weights_call(where, both, mix, act, hid, kv):
    n, width = mix.shape
    ff = kv.shape[0]
    rows = 2 * LANES
    chips = n // rows
    shape = jax.ShapeDtypeStruct
    pair = pl.BlockSpec((1, LANES, width), lambda i: (i, 0, 0))
    hidden = pl.BlockSpec((rows, ff), lambda i: (i, 0))
    return pl.pallas_call(
        ffn_weights_kernel,
        grid=(chips,),
        in_specs=[
            pl.BlockSpec(memory_space=pltpu.SMEM),
            gathered(1, width),
            pl.BlockSpec((rows, width), lambda i: (i, 0)),
            hidden,
            hidden,
            pl.BlockSpec((ff, width), lambda i: (0, 1)),
        ],
        out_specs=[pair, pair, whole(kv.shape)],
        out_shape=[shape((chips, LANES, width), BF)] * 2 + [shape(kv.shape, BF)],
        scratch_shapes=[pltpu.VMEM((width, ff), F32), pltpu.VMEM((ff, width), F32)],
        compiler_params=params(),
        cost_estimate=cost(8),
        name="ffn_weights",
    )(where, both, mix, act, hid, kv)


def ffn_call(where, both, mine, other, wo_mine, wo_other, kv, vec):
    n, width = both.shape[0] * LANES, both.shape[-1]
    ff = kv.shape[0]
    rows = 2 * LANES
    chips = n // rows
    shape = jax.ShapeDtypeStruct
    heads = pl.BlockSpec((mine.shape[0], rows, LANES), lambda i: (0, i, 0))
    outs = [
        shape((chips, LANES + EDGE, width), BF),
        shape((chips, LANES + EDGE, width), BF),
        shape((rows, width), F32),
        shape((width, width), BF),
        shape((n, width), BF),
        shape((n, ff), BF),
        shape((n, ff), BF),
    ]
    hidden = pl.BlockSpec((rows, ff), lambda i: (i, 0))
    return pl.pallas_call(
        ffn_kernel,
        grid=(chips,),
        in_specs=[
            pl.BlockSpec(memory_space=pltpu.SMEM),
            gathered(0, width),
            heads,
            heads,
            gathered(1, width),
        ]
        + [whole(a.shape) for a in (wo_mine, wo_other, kv, vec)],
        out_specs=[whole(a.shape) for a in outs[:4]]
        + [pl.BlockSpec((rows, width), lambda i: (i, 0)), hidden, hidden],
        out_shape=outs,
        scratch_shapes=[pltpu.VMEM((8, width), F32), pltpu.VMEM((width, ff), BF)],
        compiler_params=params(),
        cost_estimate=cost(14),
        name="ffn",
    )(where, both, mine, other, both, wo_mine, wo_other, kv, vec)


def norm_back(q, unit, rstd):
    return rstd * (
        q
        - jnp.mean(q, -1, keepdims=True)
        - unit * jnp.mean(q * unit, -1, keepdims=True)
    )


def add_next(grad, coef, edge):
    kept = shift_up(grad)
    last = iota(grad.shape, 0) == grad.shape[0] - 1
    return grad * (1.0 - coef) + jnp.where(last, edge, kept) * coef


def resid_kernel(
    where_ref, back_ref, resid_ref, cot_ref, mine_ref, other_ref, wo_ref, vec_ref, *rest
):
    gres_ref, gin_ref, keep_ref, give_ref, sums_ref = rest
    rows = cot_ref.shape[0]
    width = cot_ref.shape[1]
    total = jnp.sum(back_ref[...].astype(F32), 0)
    grad = total[:rows]
    position = where_ref[0] * rows + iota((rows, 1), 0)
    g_out = jnp.where(position < where_ref[1], cot_ref[...].astype(F32), 0.0)
    coef = vec_ref[12:13]
    unit, rstd = norm_parts(resid_ref[0:rows])
    normed = unit * vec_ref[1:2] + vec_ref[4:5]
    before, _ = norm_parts(resid_ref[2 * rows - 8 :])
    before = before * vec_ref[1:2] + vec_ref[4:5]
    first = jnp.where(where_ref[0] > 0, before[7:8], 0.0)
    prev = shift_down(normed, first)
    g_coef = jnp.sum((prev - normed) * grad, 0, keepdims=True)
    g_normed = add_next(grad, coef, total[rows : rows + 1])
    g_gain = jnp.sum(g_normed * unit, 0, keepdims=True)
    g_bias = jnp.sum(g_normed, 0, keepdims=True)
    g_resid = g_out + norm_back(g_normed * vec_ref[1:2], unit, rstd)
    gres_ref[...] = g_resid
    g_attn = g_resid.astype(BF)
    g_in = nt(g_attn, wo_ref[...]).astype(BF)
    core = where_ref[2]
    for q in range(gin_ref.shape[0] // 2):
        for c in range(2):
            head = 2 * q + (c + core) % 2
            gin_ref[head] = g_in[:, (2 * q + c) * LANES : (2 * q + c + 1) * LANES]
    chips, _, own, _ = keep_ref.shape
    for q in range(chips):
        for c, ref in enumerate((mine_ref, other_ref)):
            head = 2 * q + (c + core) % 2
            gwo = tn(ref[q], g_attn)
            for i in range(0, LANES // own, 2):
                owner = head * (LANES // own) + i
                even = gwo[i * own : (i + 1) * own]
                odd = gwo[(i + 1) * own : (i + 2) * own]
                chip = owner % (2 * chips) // 2
                place = owner // (2 * chips)
                keep_ref[chip, place] = jnp.where(core == 0, even, odd).astype(BF)
                give_ref[chip, place] = jnp.where(core == 0, odd, even).astype(BF)
    sums_ref[...] = jnp.concatenate(
        [g_gain, g_bias, g_coef, jnp.zeros((5, width), F32)], 0
    )


def resid_call(where, back, resid, cot, mine, other, wo, vec, dp):
    rows, width = cot.shape
    chips = mine.shape[0]
    shape = jax.ShapeDtypeStruct

    def fixed(shape):
        return pl.BlockSpec(shape, lambda i, at: (0,) * len(shape))

    heads = pl.BlockSpec((chips, rows, LANES), lambda i, at: (0, at[0], 0))
    share = shape((chips, dp, width // (2 * chips * dp), width), BF)
    outs = [
        shape((rows, width), F32),
        shape((2 * chips, rows, LANES), BF),
        share,
        share,
        shape((8, width), F32),
    ]
    return pl.pallas_call(
        resid_kernel,
        grid_spec=pltpu.PrefetchScalarGridSpec(
            num_scalar_prefetch=1,
            grid=(1,),
            in_specs=[fixed(a.shape) for a in (back, resid, cot)]
            + [heads, heads]
            + [fixed(a.shape) for a in (wo, vec)],
            out_specs=[fixed(a.shape) for a in outs],
        ),
        out_shape=outs,
        compiler_params=params(),
        cost_estimate=cost(6),
        name="resid_back",
    )(where, back, resid, cot, mine, other, wo, vec)


def recur_back_kernel(
    r_ref, k_ref, v_ref, lw_ref, rate_ref, gv_ref, own_ref, wkv_ref, w0_ref, uv_ref, *rest
):
    inv_ref, q0_ref, st_ref, d_ref, gin_ref, g_ref, sums_ref, dstate, acc = rest
    m0, m1 = lanes(LANES)

    @pl.when(pl.program_id(0) == 0)
    def _():
        dstate[...] = jnp.zeros_like(dstate)
        acc[...] = jnp.zeros_like(acc)

    count = r_ref.shape[0] // LANES
    at = [slice(c * LANES, (c + 1) * LANES) for c in range(count)]
    small = [slice(c * STATE, (c + 1) * STATE) for c in range(count)]
    r, kraw, v, rate, gv, lw, g_in = [
        [ref[q].astype(F32) for q in at]
        for ref in (r_ref, k_ref, v_ref, rate_ref, gv_ref, lw_ref, gin_ref)
    ]
    gain, bias, own_w = own_ref[5:6], own_ref[6:7], own_ref[4:5]
    mean = 1.0 / HEAD_SIZE
    parts = [key_parts(a, c, own_ref, m0, m1) for a, c in zip(kraw, rate)]
    unit, rs, keys = [[q[i] for q in parts] for i in range(3)]
    norms = [group_norm(wkv_ref[q], m0, m1) for q in at]
    normed, rstd = [q[0] for q in norms], [q[1] for q in norms]
    bonus = each(lambda a, c: head_sum(a * c * own_w, m0, m1), r, keys)
    g_gv = each(
        lambda g, a, c, d: g * (a * gain + bias + c * d), g_in, normed, bonus, v
    )
    g_pre = each(jnp.multiply, g_in, gv)
    g_norm = each(lambda a: a * gain, g_pre)
    d_out = each(
        lambda a, c, g: a
        * (g - head_sum(g, m0, m1) * mean - c * (head_sum(g * c, m0, m1) * mean)),
        rstd,
        normed,
        g_norm,
    )
    g_bonus = each(lambda a, c: head_sum(a * c, m0, m1), g_pre, v)
    local = [compact(mm(a, q0_ref[q], 0, 0), m0, m1) for a, q in zip(d_out, at)]
    ds = dstate[...]
    ends = [None] * count
    for c in reversed(range(count)):
        ends[c] = ds
        ds = local[c] + mm(ds, halves(d_ref[small[c]], m0, m1), 1, 1, PASSES)
    dstate[...] = ds
    outs = bwd_chunks(
        r,
        keys,
        v,
        unit,
        each(jnp.multiply, unit, rate),
        lw,
        [inv_ref[q] for q in at],
        [w0_ref[q] for q in at],
        [uv_ref[q] for q in at],
        d_out,
        [st_ref[q] for q in small],
        ends,
        PASSES,
    )
    ks1 = own_ref[3:4]
    sums = acc[...]
    for c in range(count):
        dr, dk, dv, dkk, db, glw = outs[c]
        dr = dr + g_bonus[c] * keys[c] * own_w
        dv = dv + g_pre[c] * bonus[c]
        dk = dk + g_bonus[c] * r[c] * own_w
        g_unit = dkk + db * rate[c]
        g_rate = db * unit[c] + dk * kraw[c] * ks1
        g_scaled = rs[c] * (g_unit - unit[c] * head_sum(g_unit * unit[c], m0, m1))
        g_kraw = dk * (1.0 + (rate[c] - 1.0) * ks1) + g_scaled * own_ref[2:3]
        g_rl = g_rate * rate[c] * (1.0 - rate[c])
        g_dl = glw * lw[c] * (1.0 + lw[c] * E_HALF)
        for j, item in enumerate((dr, g_kraw, dv, g_dl, g_rl, g_gv[c])):
            g_ref[at[c], j * LANES : (j + 1) * LANES] = item.astype(BF)
        rows = [
            g_dl,
            g_rl,
            g_scaled * kraw[c],
            dk * kraw[c] * (rate[c] - 1.0),
            g_bonus[c] * r[c] * keys[c],
            g_pre[c] * normed[c],
            g_pre[c],
        ]
        rows = [jnp.sum(item, 0, keepdims=True) for item in rows]
        sums = sums + jnp.concatenate(rows + [jnp.zeros((1, LANES), F32)], 0)
    acc[...] = sums
    sums_ref[...] = sums


def mix_part(where_ref, g_ref, h_ref, wc_ref, up_ref, keep_ref, give_ref, all_ref, carry):
    step = pl.program_id(0)
    width = wc_ref.shape[0] // 2
    core = where_ref[2]
    m0, _ = lanes(LANES)

    @pl.when(step == 0)
    def _():
        carry[...] = jnp.zeros_like(carry)

    g_dl, g_rl, g_gv = [g_ref[:, block_of(j)] for j in range(3, 6)]
    act = low_act(h_ref[:, :LANES], m0)
    sig = jax.nn.sigmoid(h_ref[:, LANES:])
    up0, up1 = up_ref[:, :LANES], up_ref[:, LANES:]
    low = jnp.where(m0 > 0, nn(g_dl, up0) * (1.0 - act * act), nn(g_rl, up0)).astype(BF)
    low_g = (nn(g_gv, up1) * sig * (1.0 - sig)).astype(BF)
    grads = jnp.concatenate([g_ref[:, : 3 * LANES], low, low_g], 1)
    all_ref[...] = grads
    later = nt(grads, wc_ref[width:])
    total = (nt(grads, wc_ref[:width]) - later + shift_up(later)).astype(BF)
    blank = jnp.zeros((EDGE, width), BF)
    count = grads.shape[0] // (2 * LANES)
    for i in range(count):
        low, mid, high = 2 * i * LANES, (2 * i + 1) * LANES, (2 * i + 2) * LANES
        chip = (pl.num_programs(0) - 1 - step) * count + i
        write_pair(keep_ref, give_ref, chip, core, total[low:mid], total[mid:high])
        edge = carry[...] if i == count - 1 else blank

        @pl.when(core == 0)
        def _(chip=chip, edge=edge):
            keep_ref[chip, LANES:] = blank
            give_ref[chip, LANES:] = edge

        @pl.when(core != 0)
        def _(chip=chip, edge=edge):
            keep_ref[chip, LANES:] = edge
            give_ref[chip, LANES:] = blank

    carry[...] = later[:EDGE].astype(BF)


def back_kernel(where_ref, h_ref, wc_ref, up_ref, *rest):
    given, (g_ref, sums_ref), outs = rest[:15], rest[15:17], rest[17:20]
    dstate, acc, grads, carry = rest[20:]
    recur_back_kernel(*given, grads, sums_ref, dstate, acc)
    g_ref[...] = grads[:, 3 * LANES :]
    mix_part(where_ref, grads, h_ref, wc_ref, up_ref, *outs, carry)


def back_call(where, h, wc, up, r, k, v, lw, rate, gv, own, wkv, w0, uv, inverse, q0, states, d, gin):
    n = r.shape[0]
    width = wc.shape[0] // 2
    c = LANES * CHUNKS
    last = n // c - 1
    chips = n // (2 * LANES)

    def rows(count, columns):
        return pl.BlockSpec((count, columns), lambda i: (last - i, 0))

    block, double, state = rows(c, LANES), rows(c, 2 * LANES), rows(CHUNKS * STATE, LANES)
    shape = jax.ShapeDtypeStruct
    pair = shape((chips, LANES + EDGE, width), BF)
    return pl.pallas_call(
        back_kernel,
        grid=(n // c,),
        in_specs=[pl.BlockSpec(memory_space=pltpu.SMEM), double]
        + [whole(wc.shape), whole(up.shape)]
        + [block] * 6
        + [whole(own.shape)]
        + [block] * 3
        + [double, block, state, state, block],
        out_specs=[rows(c, 3 * LANES), whole((8, LANES))]
        + [whole(pair.shape)] * 2
        + [rows(c, BLOCKS * LANES)],
        out_shape=[
            shape((n, 3 * LANES), BF),
            shape((8, LANES), F32),
            pair,
            pair,
            shape((n, BLOCKS * LANES), BF),
        ],
        scratch_shapes=[
            pltpu.VMEM((STATE, LANES), F32),
            pltpu.VMEM((8, LANES), F32),
            pltpu.VMEM((c, 6 * LANES), BF),
            pltpu.VMEM((EDGE, width), BF),
        ],
        compiler_params=params(),
        cost_estimate=cost(20),
        name="back",
    )(where, h, wc, up, r, k, v, lw, rate, gv, own, wkv, w0, uv, inverse, q0, states, d, gin)


VEC_ROWS = 32


def weights_back_kernel(
    where_ref, x_ref, all_ref, g_ref, h_ref, wc_ref, vec_ref, sums1_ref, sums2_ref, *rest
):
    out_ref, *rest = rest
    gw_ref, pack_ref, carry, acc_u, acc_d, acc_up, ends, vecs = rest
    step = pl.program_id(0)
    width = x_ref.shape[-1]
    m0, m1 = lanes(LANES)

    @pl.when(step == 0)
    def _():
        for item in (carry, acc_u, acc_d, acc_up, ends):
            item[...] = jnp.zeros_like(item)

    unit, _ = norm_parts(rows_of(x_ref).astype(F32))
    change = shift_down(unit, carry[0:1]) - unit
    carry[...] = jnp.broadcast_to(unit[-1:], carry.shape)
    g_dl, g_rl, g_gv = [g_ref[:, block_of(j)] for j in range(3)]
    act = low_act(h_ref[:, :LANES], m0)
    sig = jax.nn.sigmoid(h_ref[:, LANES:])
    grads = all_ref[...]
    acc_u[...] += tn(unit, grads)
    acc_d[...] += tn(change, grads)
    rounded = act.astype(BF).astype(F32)
    acc_up[:, :LANES] += tn(g_dl, rounded * m0) + tn(g_rl, rounded * m1)
    acc_up[:, LANES:] += tn(g_gv, sig)
    ends[0:1] += jnp.sum(grads.astype(F32), 0, keepdims=True)

    @pl.when(step == 0)
    def _():
        ends[1:2] = grads[0:1].astype(F32)

    @pl.when(step == pl.num_programs(0) - 1)
    def _():
        seq = pack_ref.shape[0]
        dp = gw_ref.shape[0]
        own = width // (seq * dp)
        wo = jnp.sum(out_ref[...].astype(F32), 0).astype(BF)
        for i in range(dp):
            gw_ref[i, 3 * own :] = wo[i * own : (i + 1) * own]
        gain, bias = column(vec_ref, 0), column(vec_ref, 3)
        coefs = mix_columns(vec_ref)
        lane = iota((1, LANES), 1)
        found = jnp.zeros((width, LANES), F32)
        g_gain = jnp.zeros((width, 1), F32)
        g_bias = jnp.zeros((width, 1), F32)
        for j in range(BLOCKS):
            at = block_of(j)
            plain = wc_ref[:width, at].astype(F32)
            mixed = wc_ref[width:, at].astype(F32)
            u, d = acc_u[:, at], acc_d[:, at]
            total, first = ends[0:1, at], ends[1:2, at]
            b = gain * d - bias * first
            grad = (gain * u + bias * total + coefs[:, at] * b).astype(BF)
            for i in range(dp):
                for s in range(seq):
                    rows = slice((i * seq + s) * own, (i * seq + s + 1) * own)
                    if j < 3:
                        gw_ref[i, j * own : (j + 1) * own, block_of(s)] = grad[rows]
                    else:
                        row = (2 * i + j - 3) * own
                        pack_ref[s, row : row + own] = grad[rows]
            shift = plain * b
            g_gain += jnp.sum(plain * u + mixed * d, -1, keepdims=True)
            g_bias += jnp.sum(plain * total - mixed * first, -1, keepdims=True)
            if j == 3:
                found += jnp.where(lane == 1, jnp.sum(shift * m0, -1, keepdims=True), 0.0)
                found += jnp.where(lane == 4, jnp.sum(shift * m1, -1, keepdims=True), 0.0)
            else:
                where = (0, 2, 3, None, 5)[j]
                found += jnp.where(lane == where, jnp.sum(shift, -1, keepdims=True), 0.0)
        found += jnp.where(lane == 6, g_gain, 0.0) + jnp.where(lane == 7, g_bias, 0.0)
        for tile in range(width // LANES):
            vecs[0:8, block_of(tile)] = found[block_of(tile)].T[0:8]
        vecs[8:16] = sums1_ref[...]
        vecs[16:24] = jnp.zeros((8, width), F32)
        vecs[16:24, pl.ds(pl.multiple_of(where_ref[0] * LANES, LANES), LANES)] = sums2_ref[...]
        owners = LANES // own
        base = 2 * dp * own
        up_grad = acc_up[...].astype(BF)
        for s in range(seq):
            for j in range(2):
                i = s % owners
                pack_ref[s, base + j * own : base + (j + 1) * own] = up_grad[
                    i * own : (i + 1) * own, block_of(j)
                ]
            out = jnp.zeros((24, LANES), F32)
            for i in range(dp):
                source = i * seq + s
                tile = vecs[:, block_of(source // owners)]
                turned = pltpu.roll(tile, (i - source % owners) * own % LANES, 1)
                out = jnp.where(lane // own == i, turned, out)
            out = jnp.concatenate([out, jnp.zeros((VEC_ROWS - 24, LANES), F32)], 0)
            pack_ref[s, base + 2 * own :] = out.astype(BF)


def weights_back_call(where, x, grads, g, h, wc, up, vec, sums1, sums2, sums_out, dp):
    seq, width = x.shape[0], x.shape[-1]
    n = seq * LANES
    rows = 2 * LANES
    own = width // (seq * dp)
    shape = jax.ShapeDtypeStruct
    outs = [
        shape((dp, 4 * own, width), BF),
        shape((seq, 2 * dp * own + 2 * own + VEC_ROWS, LANES), BF),
    ]
    return pl.pallas_call(
        weights_back_kernel,
        grid=(n // rows,),
        in_specs=[
            pl.BlockSpec(memory_space=pltpu.SMEM),
            gathered(0, width),
            pl.BlockSpec((rows, BLOCKS * LANES), lambda i: (i, 0)),
            pl.BlockSpec((rows, 3 * LANES), lambda i: (i, 0)),
            pl.BlockSpec((rows, 2 * LANES), lambda i: (i, 0)),
        ]
        + [whole(a.shape) for a in (wc, vec, sums1, sums2)]
        + [pl.BlockSpec((sums_out.shape[0], LANES, width), lambda i: (0, 1, 0))],
        out_specs=[whole(a.shape) for a in outs],
        out_shape=outs,
        scratch_shapes=[
            pltpu.VMEM((8, width), F32),
            pltpu.VMEM((width, BLOCKS * LANES), F32),
            pltpu.VMEM((width, BLOCKS * LANES), F32),
            pltpu.VMEM(up.shape, F32),
            pltpu.VMEM((8, BLOCKS * LANES), F32),
            pltpu.VMEM((24, width), F32),
        ],
        compiler_params=params(),
        cost_estimate=cost(10),
        name="weights_back",
    )(where, x, grads, g, h, wc, vec, sums1, sums2, sums_out)


def pack_kernel(where_ref, pack_ref, out_ref):
    dp, own, _ = out_ref.shape
    pair = 2 * own
    base = dp * pair
    owners = dp
    total = jnp.sum(pack_ref[...].astype(F32), 0)
    for d in range(dp):
        source = d * (pack_ref.shape[0] // dp) + where_ref[0] // owners
        down = total[d * pair : (d + 1) * pair].astype(BF)
        up = pack_ref[source, base : base + pair]
        vec = total[base + pair :].astype(BF)
        parts = (down[:own], down[own:], up[:own], up[own:], vec)
        for j, part in enumerate(parts):
            out_ref[d, :, block_of(j)] = part


def pack_call(where, pack, dp):
    own = (pack.shape[1] - VEC_ROWS) // (dp + 1) // 2
    vm = pl.BlockSpec(memory_space=pltpu.VMEM)
    return pl.pallas_call(
        pack_kernel,
        in_specs=[pl.BlockSpec(memory_space=pltpu.SMEM), vm],
        out_specs=vm,
        out_shape=jax.ShapeDtypeStruct((dp, own, 5 * LANES), BF),
        compiler_params=pltpu.CompilerParams(vmem_limit_bytes=16 << 20),
        cost_estimate=cost(2),
        name="pack_sums",
    )(where, pack)


def finish_kernel(cuts, where_ref, pack_ref, *outs):
    own = outs[0].shape[0]
    total = jnp.sum(pack_ref[...].astype(F32), 0)
    first, second, up_first, up_second, vec = [total[:, block_of(j)] for j in range(5)]
    up_first, up_second = up_first.T, up_second.T
    vec = pltpu.roll(vec, (LANES - where_ref[3] * own) % LANES, 1)[:, :own]
    cut0, cut1 = cuts
    pieces = (
        first[:, :cut0],
        up_first[:cut0],
        first[:, cut0:cut1],
        up_first[cut0:cut1],
        second,
        up_second,
        jnp.concatenate([vec[6:7], vec[8:9], vec[21:22]], 0),
        jnp.concatenate([vec[7:8], vec[9:10], vec[22:23]], 0),
        jnp.concatenate([vec[0:1], vec[2:6], vec[10:11]], 0),
        vec[1:2],
        vec[16:17],
        vec[17:18],
        vec[18:20],
        vec[20:21],
    )
    for ref, piece in zip(outs, pieces):
        ref[...] = piece.reshape(ref.shape)


def finish_call(where, pack, ranks, own):
    down0, down1, down2 = ranks
    shapes = [
        (own, down0),
        (down0, own),
        (own, down1),
        (down1, own),
        (own, down2),
        (down2, own),
        (3, own),
        (3, own),
        (6, own),
        (own,),
        (own,),
        (own,),
        (2, own),
        (own,),
    ]
    vm = pl.BlockSpec(memory_space=pltpu.VMEM)
    return pl.pallas_call(
        partial(finish_kernel, (down0, down0 + down1)),
        in_specs=[pl.BlockSpec(memory_space=pltpu.SMEM), vm],
        out_specs=[vm] * len(shapes),
        out_shape=[jax.ShapeDtypeStruct(shape, F32) for shape in shapes],
        compiler_params=pltpu.CompilerParams(vmem_limit_bytes=16 << 20),
        cost_estimate=cost(2),
        name="finish",
    )(where, pack)


def input_kernel(back_ref, x_ref, gres_ref, vec_ref, out_ref):
    rows = x_ref.shape[0]
    total = jnp.sum(back_ref[...].astype(F32), 0)
    grad = total[:rows]
    last = iota(grad.shape, 0) == rows - 1
    grad = grad + jnp.where(last, total[rows : rows + 1], 0.0)
    unit, rstd = norm_parts(rows_of(x_ref).astype(F32))
    out = gres_ref[...] + norm_back(grad * vec_ref[0:1], unit, rstd)
    out_ref[...] = out.astype(BF)


def input_call(back, x, gres, vec):
    vm = pl.BlockSpec(memory_space=pltpu.VMEM)
    return pl.pallas_call(
        input_kernel,
        in_specs=[vm] * 4,
        out_specs=vm,
        out_shape=jax.ShapeDtypeStruct(x.shape, BF),
        compiler_params=pltpu.CompilerParams(vmem_limit_bytes=56 << 20),
        cost_estimate=cost(3),
        name="input_back",
    )(back, x, gres, vec)


def exchange(x, axis):
    return lax.all_to_all(x, axis, 0, 0, tiled=True)


def swap_cores(x):
    return lax.ppermute(x, "core", [(0, 1), (1, 0)])


def copies(x, axis):
    return jnp.broadcast_to(x[None], (lax.axis_size(axis),) + x.shape)


def spread(stacked, axis="chip"):
    mine = exchange(stacked, axis)
    return mine, swap_cores(mine)


def add_cores(keep, give):
    return (keep.astype(F32) + swap_cores(give).astype(F32)).astype(BF)


def after(x, *others):
    return lax.optimization_barrier((x,) + others)[0]


def local_slot(
    tokens,
    lengths,
    cotangent,
    attention_weights,
    output_weight,
    decay_down_matrix,
    decay_up_matrix,
    rate_down_matrix,
    rate_up_matrix,
    gate_down_matrix,
    gate_up_matrix,
    feedforward_key,
    feedforward_value,
    layer_norm_gains,
    layer_norm_biases,
    shift_coefficients,
    decay_offset_base,
    rate_logit_base,
    removal_key_scales,
    own_term_weights,
):
    dp, seq = lax.axis_size("dp"), lax.axis_size(SEQ)
    rank = lax.axis_index(SEQ)
    rows, width = tokens.shape[1:]
    devices = dp * seq
    own = width // devices
    ff = feedforward_key.shape[1]
    my_tokens, my_cot = tokens[0], cotangent[0]
    where = jnp.stack([rank.astype(jnp.int32), lengths[0]])

    both = lax.all_gather(jnp.stack([my_tokens, my_cot]), SEQ)
    downs = jnp.concatenate([decay_down_matrix, rate_down_matrix, gate_down_matrix], 1)
    ups = jnp.concatenate([decay_up_matrix, rate_up_matrix, gate_up_matrix], 0).T
    low = downs.shape[1]
    low_rows = 2 * own
    owners = LANES // own
    heads_w = jnp.moveaxis(attention_weights.reshape(3, own, seq, LANES), 2, 0)
    vectors = jnp.concatenate(
        [
            layer_norm_gains,
            layer_norm_biases,
            shift_coefficients,
            decay_offset_base[None],
            rate_logit_base[None],
            removal_key_scales,
            own_term_weights[None],
        ],
        0,
    )
    count = vectors.shape[0]
    vec_rows = as_rows(vectors.reshape(-1), LANES * 8).reshape(-1, LANES)
    part_rows = feedforward_value.shape[0]
    key = feedforward_key.reshape(own, dp, seq, part_rows)
    key = jnp.transpose(key, (2, 1, 0, 3)).reshape(seq, dp * own, part_rows)
    cut = 3 * own
    heads = exchange(
        jnp.concatenate(
            [heads_w.reshape(seq, -1, LANES), copies(ups[:, :LANES], SEQ), key], 1
        ),
        SEQ,
    )
    small = jnp.concatenate(
        [downs[:, :LANES], downs[:, LANES:], ups[:, LANES:], vec_rows]
        + [output_weight[:, block_of(j)] for j in range(width // LANES)],
        0,
    )
    small = lax.all_gather(small, "dp")
    heads = after(heads, small)
    group = owners * (rank % (seq // dp))
    home = rank // (seq // dp)
    mine_up = lax.dynamic_slice_in_dim(heads[:, cut : cut + own], group, owners, 0)
    flat = jnp.concatenate(
        [heads[:, :cut].reshape(-1, LANES), mine_up.reshape(-1, LANES)], 0
    )
    key = heads[:, cut + own :].reshape(seq, dp, own, part_rows)
    key = jnp.transpose(key, (0, 2, 1, 3)).reshape(2, part_rows, dp * part_rows)
    kv = jnp.concatenate([key[0], key[1], feedforward_value], 1)
    flat, kv = lax.optimization_barrier((flat, kv))
    kv = lax.all_gather(kv, "dp", tiled=True)
    flat = lax.all_gather(flat, "dp")
    split = low_rows + own + vec_rows.shape[0]
    wo_part = small[:, split:].reshape(dp, width // LANES, own, LANES)
    first = exchange(copies(small[:, :split], SEQ), SEQ)
    up_low = lax.dynamic_index_in_dim(flat[:, seq * cut :], home, 0, False)
    up_gate = first[:, :, low_rows : low_rows + own]
    up_gate = lax.dynamic_slice(up_gate, (group, home, 0, 0), (owners, 1, own, LANES))
    up = jnp.concatenate([up_low, up_gate.reshape(LANES, LANES)], 1)
    wo_part, flat, first = lax.optimization_barrier((wo_part, flat, first))
    wo_mine = exchange(copies(wo_part, "chip"), "chip")
    start = rank * LANES
    vec = first[:, :, low_rows + own :].reshape(seq, dp, -1)[:, :, : count * own]
    vec = jnp.transpose(vec.reshape(seq, dp, count, own), (2, 1, 0, 3))
    vec = vec.reshape(count, width).astype(F32)
    own_vec = lax.dynamic_slice_in_dim(vec, start, LANES, 1)
    own_vec = jnp.concatenate(
        [own_vec[13:18], own_vec[2:3], own_vec[5:6], jnp.zeros((1, LANES), F32)], 0
    )
    core = lax.axis_index("core")
    where = [rank, lengths[0], core, lax.axis_index("dp")]
    where = jnp.stack([item.astype(jnp.int32) for item in where])
    chips = lax.axis_size("chip")

    r, k, v, lw, rate, gv, h, wc, attn, wkv, w0, uv, inverse, q0, states, d = front_call(
        both, flat, first, up, vec, own_vec, chips
    )
    attn, wo_mine = lax.optimization_barrier((attn, wo_mine))
    wo_other = swap_cores(wo_mine)
    mine, other = spread(attn)
    mine, other, kv = lax.optimization_barrier((mine, other, kv))
    keep, give, resid, wo, ffn_mix, act, hidden_grad = ffn_call(
        where, both, mine, other, wo_mine, wo_other, kv, vec
    )
    back = exchange(add_cores(keep, give), "chip")
    keep_part, give_part, gkv = ffn_weights_call(where, both, ffn_mix, act, hidden_grad, kv)
    back, keep_part, give_part = lax.optimization_barrier((back, keep_part, give_part))
    gkv = lax.psum_scatter(gkv, "dp", scatter_dimension=0, tiled=True)
    g_resid, g_in, keep_wo, give_wo, sums1 = resid_call(
        where, back, resid, my_cot, mine, other, wo, vec, dp
    )
    g_in = exchange(g_in, SEQ)
    share = (chips, dp * own, width)
    sums_out = jnp.concatenate(
        [
            add_cores(keep_part, give_part),
            add_cores(keep_wo.reshape(share), give_wo.reshape(share)),
        ],
        1,
    )
    g_in, sums_out = lax.optimization_barrier((g_in, sums_out))
    sums_out = exchange(sums_out, "chip")
    g, sums2, keep2, give2, grads = back_call(
        where,
        h,
        wc,
        up,
        r,
        k,
        v,
        lw,
        rate,
        gv,
        own_vec,
        wkv,
        w0,
        uv,
        inverse,
        q0,
        states,
        d,
        g_in.reshape(seq * rows, LANES),
    )
    keep2, give2, sums_out = lax.optimization_barrier((keep2, give2, sums_out))
    ffn_out = sums_out[:, :rows]
    back2 = exchange(add_cores(keep2, give2), "chip")
    gw, pack = weights_back_call(
        where, both, grads, g, h, wc, up, vec, sums1, sums2, sums_out, dp
    )
    gw, pack, back2, gkv = lax.optimization_barrier((gw, pack, back2, gkv))
    gw = lax.psum_scatter(gw, "dp", scatter_dimension=0, tiled=False)
    pack = exchange(pack, SEQ)
    pack = pack_call(where, pack, dp)
    gkey = jnp.stack([gkv[:, : dp * part_rows], gkv[:, dp * part_rows : 2 * dp * part_rows]])
    gkey = gkey.reshape(seq, own, dp, part_rows).swapaxes(1, 2).reshape(seq, dp * own, part_rows)
    mix = jnp.moveaxis(gw[:cut].reshape(cut, seq, LANES), 1, 0)
    mix = jnp.concatenate([mix, gkey], 1)
    pack = exchange(pack, "dp")
    mix, pack = lax.optimization_barrier((mix, pack))
    mix = exchange(mix, SEQ)
    input_grad = input_call(back2, my_tokens, g_resid, vec)
    ranks = (decay_down_matrix.shape[1], rate_down_matrix.shape[1], gate_down_matrix.shape[1])
    ends = finish_call(where, pack, ranks, own)
    mix_sum = mix[:, :cut].reshape(seq, 3, own, LANES)
    mix_sum = jnp.transpose(mix_sum, (1, 2, 0, 3)).reshape(3, own, width).astype(F32)
    key_sum = mix[:, cut:].reshape(seq, dp, own, part_rows)
    key_sum = jnp.transpose(key_sum, (2, 1, 0, 3)).reshape(own, ff).astype(F32)
    ffn_out = jnp.sum(ffn_out.astype(F32), 0)
    position = rank * rows + jnp.arange(rows, dtype=jnp.int32)
    valid = (position < lengths[0]).astype(F32)[:, None]
    output = (valid * (resid[:rows] + ffn_out)).astype(BF)
    value_sum = gkv[:, 2 * dp * part_rows :].astype(F32)
    wo_sum = gw[cut:].astype(F32)
    return (
        output[None],
        input_grad[None],
        mix_sum,
        wo_sum,
        *ends[:6],
        key_sum,
        value_sum,
        *ends[6:],
    )


def specs_of(axes):
    both = axes
    seq = axes[1:] if len(axes) > 2 else axes[1]
    row = P("dp", seq, None)
    first = P(both, None)
    second = P(None, both)
    vector = P(both)
    ins = (row, P("dp"), row, P(None, both, None)) + (first,)
    ins += (first, second, first, second, first, second, first, first)
    ins += (second, second, second, vector, vector, second, vector)
    outs = (row, row, P(None, both, None), first)
    outs += (first, second, first, second, first, second, first, first)
    outs += (second, second, second, vector, vector, vector, second, vector)
    return ins, outs


def solution(mesh):
    dp, seq = mesh.shape["dp"], mesh.shape["seq"]
    by_heads = HEADS * HEAD_SIZE // seq == LANES
    if by_heads:
        mesh = Mesh(mesh.devices.reshape(dp, seq // 2, 2), ALL)
    ins, outs = specs_of(ALL if by_heads else BOTH)
    run = local_slot if by_heads else local
    return jax.shard_map(run, mesh=mesh, in_specs=ins, out_specs=outs, check_vma=False)
```
